32 devices in a mesh: expert: 8 (over z, x), dp: 2 (over core), tensor: 2 (over y).
Axes of the slice: x: 2, y: 2, z: 4, core: 2. Of those that a mesh axis runs over, the one named last changes fastest.
Arguments:
- tokens: bfloat16 [3072, 3584], P(('expert', 'dp'), 'tensor'), may hold values from -6 to 6
- routes: int32 [3072, 8], P(('expert', 'dp')), may hold values from 0 to 255, all different within a row
- gates: bfloat16 [3072, 8], P(('expert', 'dp')), may hold values from 0.049804688 to 1
- cotangent: bfloat16 [3072, 3584], P(('expert', 'dp'), 'tensor'), may hold values from -6 to 6
- placement: int32 [8], replicated, may hold values from 0 to 7, each once
- swap_flag: int32 [8], replicated, may hold values from 0 to 1, as said below
- w_gate: bfloat16 [8, 3584, 1024], P('expert', 'dp', 'tensor'), may hold values from -0.09375 to 0.09375
- w_up: bfloat16 [8, 3584, 1024], P('expert', 'dp', 'tensor'), may hold values from -0.09375 to 0.09375
- w_down: bfloat16 [8, 3584, 1024], P('expert', 'dp', 'tensor'), may hold values from -0.1875 to 0.1875
Outputs:
- layer_out: bfloat16 [3072, 3584], P(('expert', 'dp'), 'tensor')
- input_grad: bfloat16 [3072, 3584], P(('expert', 'dp'), 'tensor')
- gate_grad: float32 [3072, 8], P(('expert', 'dp'))
- grad_gate_w: bfloat16 [8, 3584, 1024], P('expert', 'dp', 'tensor')
- grad_up_w: bfloat16 [8, 3584, 1024], P('expert', 'dp', 'tensor')
- grad_down_w: bfloat16 [8, 3584, 1024], P('expert', 'dp', 'tensor')
The draws below stay inside these ranges and needn't reach their ends.
Inputs may be any that keep to these rules, and one draw needn't show every extreme that they name: `swap_flag`: entry i equals entry (i + 4) mod 8; some pair has 1 and some pair 0. `placement`: a permutation of the positions. `routes`: each row names 8 different experts.
All inputs are finite; a program needn't handle non-finite values.
Results may differ from the reference program's by a relative error of at most 0.0095.
Values may be sent and summed in bfloat16 or wider, within the bound.
No kernel may reach another device: no remote copies, remote signals or barrier semaphores. Data moves between devices by JAX's collectives and lax.ppermute only.
A program may use at most 128 MiB of HBM per device.

```python
import math
import jax
import jax.numpy as jnp
from jax import lax

D = 3584
HID = 1024
ROUTED = 256
TOPK = 8
TOK_DEV = 192
CAP = 9
TOKENS = 3072
N_EXPERT = 8
N_DP = 2
N_TENSOR = 2


def draw_swap_flag(key, part):
    pairs = N_EXPERT // 2
    first, second, third = jax.random.split(key, 3)
    flags = jax.random.randint(first, (pairs,), 0, 2)
    chosen = jax.random.randint(second, (), 0, pairs)
    other = (chosen + 1 + jax.random.randint(third, (), 0, pairs - 1)) % pairs
    flags = flags.at[chosen].set(1).at[other].set(0)
    return jnp.concatenate([flags, flags]).astype(jnp.int32)


def shard_levels(key, dims, pieces, least, high):
    factor_of, own = 1.0, jax.random.fold_in(key, 6)
    for position, shards_of in pieces:
        draws = jnp.exp(jax.random.uniform(jax.random.fold_in(own, position), (shards_of,), jnp.float32, least / len(pieces), high / len(pieces)))
        factor_of = factor_of * jnp.repeat(draws, dims[position] // shards_of).reshape([-1 if axis == position else 1 for axis in range(len(dims))])
    return factor_of


def different_ones(own_key, rows, amount, top, lift):
    sequence = jax.random.permutation(jax.random.fold_in(own_key, 1), amount)
    favour = sequence
    for power in range(3):
        favour = favour * favour // amount
    favour = favour * lift // amount
    chance = jax.random.randint(jax.random.fold_in(own_key, 2), (rows, amount), 0, 4096) + favour
    fixed_rows = jax.random.permutation(jax.random.fold_in(own_key, 3), rows)[jnp.arange(amount) % rows]
    chance = jnp.where(jnp.arange(rows)[:, None] == fixed_rows[None, :], 1 << 14, chance)
    priority = chance * amount + jnp.arange(amount)
    return lax.top_k(priority.astype(jnp.int32), top)[1].astype(jnp.int32)


def scatter_about(rng, extent, scale, most, cuts=(), kind=jnp.bfloat16):
    level = shard_levels(rng, extent, cuts, -0.22, 0.18) if cuts else 1.0
    entries = jax.random.normal(rng, extent, jnp.float32) * scale * level
    return jnp.minimum(jnp.maximum(entries, -most), most).astype(kind)


def setup_inputs(seed: int = 0) -> dict:
    key_list = jax.random.split(jax.random.key(seed), 10)
    return {
        "tokens": scatter_about(key_list[0], (TOKENS, D), 1.0, 6.0, ((0, 16), (1, 2))),
        "routes": different_ones(key_list[1], TOKENS, ROUTED, TOPK, 512),
        "gates": jnp.clip(jnp.exp(math.log(1.0) - 2.9996462 * jax.random.uniform(key_list[2], (TOKENS, TOPK), jnp.float32) ** shard_levels(key_list[2], (TOKENS, TOPK), ((0, 16),), -0.2, 0.2)), 0.049804688, 1.0).astype(jnp.bfloat16),
        "cotangent": scatter_about(key_list[3], (TOKENS, D), 1.0, 6.0, ((0, 16), (1, 2))),
        "placement": jax.random.permutation(key_list[4], N_EXPERT).astype(jnp.int32),
        "swap_flag": draw_swap_flag(jax.random.fold_in(key_list[9], 71), 0),
        "w_gate": scatter_about(key_list[6], (N_EXPERT, D, HID), D ** -0.5, 0.09375, ((0, 8), (1, 2), (2, 2))),
        "w_up": scatter_about(key_list[7], (N_EXPERT, D, HID), D ** -0.5, 0.09375, ((0, 8), (1, 2), (2, 2))),
        "w_down": scatter_about(key_list[8], (N_EXPERT, D, HID), HID ** -0.5, 0.1875, ((0, 8), (1, 2), (2, 2))),
    }


def rounded(value):
    return lax.optimization_barrier(value.astype(jnp.bfloat16)).astype(jnp.float32)


def reference(tokens, routes, gates, cotangent, placement, swap_flag, w_gate, w_up, w_down):
    experts = N_EXPERT
    places = jnp.arange(experts, dtype=jnp.int32)
    source = jnp.where(swap_flag == 1, (places + experts // 2) % experts, places)
    held = placement[source]
    gate_w = w_gate[source]
    up_w = w_up[source]
    down_w = w_down[source]
    owner_of = jnp.zeros((experts,), jnp.int32).at[held].set(places)
    inside = routes < experts
    owner = jnp.where(inside, owner_of[jnp.where(inside, routes, 0)], experts)
    groups = TOKENS // TOK_DEV
    group_pairs = TOK_DEV * TOPK
    owner_g = owner.reshape(groups, group_pairs)
    onehot = (owner_g[:, :, None] == places[None, None, :]).astype(jnp.int32)
    earlier = jnp.cumsum(onehot, axis=1) - onehot
    slot = jnp.sum(earlier * onehot, axis=2)
    kept = (owner_g < experts) & (slot < CAP)
    group_ids = jnp.broadcast_to(jnp.arange(groups, dtype=jnp.int32)[:, None], (groups, group_pairs))
    sender = group_ids // N_DP
    replica = group_ids % N_DP
    pair_ids = jnp.arange(TOKENS * TOPK, dtype=jnp.int32).reshape(groups, group_pairs)
    rows = experts * CAP
    table = jnp.full((experts, N_DP, rows), -1, jnp.int32)
    table = table.at[jnp.where(kept, owner_g, experts), replica, sender * CAP + jnp.minimum(slot, CAP - 1)].set(pair_ids, mode="drop")
    gate_flat = gates.reshape(-1)
    width = HID // N_TENSOR
    contract = (((0,), (0,)), ((), ()))
    inner = (((1,), (1,)), ((), ()))

    def per_expert(item):
        gate_e, up_e, down_e, tab = item
        outs_eo = []
        outs_dx = []
        outs_dg = []
        grad_g = jnp.zeros((D, HID), jnp.float32)
        grad_u = jnp.zeros((D, HID), jnp.float32)
        grad_d = jnp.zeros((D, HID), jnp.float32)
        for index in range(N_DP):
            pid = tab[index]
            live = pid >= 0
            safe = jnp.where(live, pid, 0)
            token_row = safe // TOPK
            inputs = jnp.where(live[:, None], tokens[token_row], jnp.zeros((), jnp.bfloat16))
            weight = jnp.where(live, gate_flat[safe], jnp.zeros((), jnp.bfloat16)).astype(jnp.float32)
            back = jnp.where(live[:, None], cotangent[token_row], jnp.zeros((), jnp.bfloat16)).astype(jnp.float32)
            pre_gate = jnp.dot(inputs, gate_e, preferred_element_type=jnp.float32)
            pre_up = jnp.dot(inputs, up_e, preferred_element_type=jnp.float32)
            sig = jax.nn.sigmoid(pre_gate)
            hidden = (pre_gate * sig * pre_up).astype(jnp.bfloat16)
            expert_out = jnp.zeros((rows, D), jnp.float32)
            for part in range(N_TENSOR):
                lo_col = part * width
                term = lax.dot_general(hidden[:, lo_col:lo_col + width], down_e[:, lo_col:lo_col + width], inner, preferred_element_type=jnp.float32)
                expert_out = expert_out + rounded(term)
            expert_out = expert_out.astype(jnp.bfloat16)
            outs_dg.append(jnp.sum(back * expert_out.astype(jnp.float32), axis=1))
            d_out = (weight[:, None] * back).astype(jnp.bfloat16)
            d_hidden = jnp.dot(d_out, down_e, preferred_element_type=jnp.float32)
            d_pre_gate = (d_hidden * pre_up * sig * (1.0 + pre_gate * (1.0 - sig))).astype(jnp.bfloat16)
            d_pre_up = (d_hidden * pre_gate * sig).astype(jnp.bfloat16)
            d_inputs = jnp.zeros((rows, D), jnp.float32)
            for part in range(N_TENSOR):
                lo_col = part * width
                term = lax.dot_general(d_pre_gate[:, lo_col:lo_col + width], gate_e[:, lo_col:lo_col + width], inner, preferred_element_type=jnp.float32)
                term = term + lax.dot_general(d_pre_up[:, lo_col:lo_col + width], up_e[:, lo_col:lo_col + width], inner, preferred_element_type=jnp.float32)
                d_inputs = d_inputs + rounded(term)
            outs_eo.append(expert_out)
            outs_dx.append(d_inputs.astype(jnp.bfloat16))
            grad_g = grad_g + rounded(lax.dot_general(inputs, d_pre_gate, contract, preferred_element_type=jnp.float32))
            grad_u = grad_u + rounded(lax.dot_general(inputs, d_pre_up, contract, preferred_element_type=jnp.float32))
            grad_d = grad_d + rounded(lax.dot_general(d_out, hidden, contract, preferred_element_type=jnp.float32))
        return (jnp.stack(outs_eo), jnp.stack(outs_dx), jnp.stack(outs_dg), grad_g.astype(jnp.bfloat16), grad_u.astype(jnp.bfloat16), grad_d.astype(jnp.bfloat16))

    eo_all, dx_all, dg_all, grad_gate_w, grad_up_w, grad_down_w = lax.map(per_expert, (gate_w, up_w, down_w, table))
    pid = table.reshape(-1)
    live = pid >= 0
    token_index = jnp.where(live, pid // TOPK, TOKENS)
    weight_all = jnp.where(live, gate_flat[jnp.where(live, pid, 0)], jnp.zeros((), jnp.bfloat16)).astype(jnp.float32)
    layer_out = jnp.zeros((TOKENS, D), jnp.float32).at[token_index].add(weight_all[:, None] * eo_all.reshape(-1, D).astype(jnp.float32), mode="drop")
    input_grad = jnp.zeros((TOKENS, D), jnp.float32).at[token_index].add(dx_all.reshape(-1, D).astype(jnp.float32), mode="drop")
    gate_grad = jnp.zeros((TOKENS * TOPK,), jnp.float32).at[jnp.where(live, pid, TOKENS * TOPK)].set(dg_all.reshape(-1), mode="drop").reshape(TOKENS, TOPK)
    return (layer_out.astype(jnp.bfloat16), input_grad.astype(jnp.bfloat16), gate_grad, grad_gate_w, grad_up_w, grad_down_w)
```

```python
import jax
import jax.numpy as jnp
from jax import lax
from jax.sharding import PartitionSpec as P

CAP = 9
BF = jnp.bfloat16
F32 = jnp.float32
LANES = 128

contract = (((0,), (0,)), ((), ()))
inner = (((1,), (1,)), ((), ()))


def dot(a, b, dims):
    return lax.dot_general(a, b, dims, preferred_element_type=F32)


def pick(stack, index, count):
    return stack[0] if count == 1 else lax.dynamic_index_in_dim(stack, index, 0, keepdims=False)


class Layout:
    def __init__(self):
        self.n_d = lax.axis_size("dp")
        self.n_t = lax.axis_size("tensor")
        self.group = self.n_d // self.n_t
        self.d = lax.axis_index("dp")
        self.t = lax.axis_index("tensor")
        self.order = (self.d % self.group) * self.n_t + self.t

    def pairs(self, step):
        route = []
        for d in range(self.n_d):
            for t in range(self.n_t):
                half = d // self.group
                data = ((d % self.group) * self.n_t + t + step) % self.n_d
                route.append((data * self.n_t + half, d * self.n_t + t))
        return route

    def canonical(self, blocks):
        if self.group == 1:
            return jnp.stack(blocks)
        whole = jnp.stack(blocks)
        return jnp.take(whole, (jnp.arange(self.n_d) - self.order) % self.n_d, axis=0)

    def spread(self, rows):
        blocks = []
        for step in range(self.n_d):
            target = (self.d - step) % self.n_d
            chunk = pick(rows, target // self.n_t, self.group)
            blocks.append(lax.ppermute(chunk, ("dp", "tensor"), self.pairs(step)))
        return self.canonical(blocks)

    def collect(self, blocks):
        parts = []
        for step in range(self.n_d):
            if self.group == 1:
                block = blocks[step]
            else:
                block = pick(blocks, (self.order + step) % self.n_d, self.n_d)
            route = [(b, a) for a, b in self.pairs(step)]
            got = lax.ppermute(block, ("dp", "tensor"), route).astype(F32)
            source = (self.d - step) % self.n_d
            parts.append(
                jnp.stack([jnp.where(source // self.n_t == c, got, 0.0) for c in range(self.group)])
                if self.group > 1
                else got[None]
            )
        total = parts[0]
        for part in parts[1:]:
            total = total + part
        return total.astype(BF)

    def summed(self, value):
        total = value
        for step in range(1, self.n_d):
            route = [(i, (i + step) % self.n_d) for i in range(self.n_d)]
            total = total + lax.ppermute(value, "dp", route)
        return total

    def gathered(self, value):
        if self.n_d == 2:
            other = lax.ppermute(value, "dp", [(0, 1), (1, 0)])
            first = self.d == 0
            return jnp.stack([jnp.where(first, value, other), jnp.where(first, other, value)])
        return lax.all_gather(value, "dp", axis=0)


def exchanged(rows, experts):
    cols = rows.shape[1]
    flat = rows.reshape(experts, CAP * cols // LANES, LANES)
    got = lax.all_to_all(flat, "expert", split_axis=0, concat_axis=0, tiled=True)
    return got.reshape(experts * CAP, cols)


def on_device(tokens, routes, gates, cotangent, placement, swap_flag, w_gate, w_up, w_down):
    experts = lax.axis_size("expert")
    myself = lax.axis_index("expert")
    lay = Layout()
    places = jnp.arange(experts, dtype=jnp.int32)
    my_flag = jnp.sum(jnp.where(places == myself, swap_flag, 0)) == 1
    wg, wu, wd = w_gate[0], w_up[0], w_down[0]
    chunk, units = wg.shape
    tok_count, top_count = routes.shape
    slots_all = experts * CAP
    half_width = tokens.shape[1]

    slot_ids = lax.broadcasted_iota(jnp.int32, (1, slots_all), 1)
    wanted = jnp.repeat(placement, CAP)[None, :]
    match = [routes[:, k : k + 1] == wanted for k in range(top_count)]
    hit = match[0]
    for m in match[1:]:
        hit = hit | m
    weight = jnp.zeros((tok_count, slots_all), F32)
    for k in range(top_count):
        weight = weight + jnp.where(match[k], gates[:, k : k + 1].astype(F32), 0.0)
    row_id = lax.broadcasted_iota(jnp.int32, (tok_count, tok_count), 0)
    col_id = lax.broadcasted_iota(jnp.int32, (tok_count, tok_count), 1)
    before = (col_id < row_id).astype(BF)
    earlier = jnp.dot(before, hit.astype(BF), preferred_element_type=F32)
    live = hit & (earlier == (slot_ids % CAP).astype(F32))
    select = live.astype(BF)
    weighted = jnp.where(live, weight, 0.0).astype(BF)

    outgoing = jnp.concatenate(
        [dot(select, tokens, contract).astype(BF), dot(weighted, cotangent, contract).astype(BF)],
        axis=1,
    )
    arrived = exchanged(outgoing, experts)

    def chunks(rows):
        both = rows.reshape(slots_all, 2, lay.group, chunk)
        if lay.group == 1:
            return rows[None]
        return jnp.moveaxis(both, 2, 0).reshape(lay.group, slots_all, 2 * chunk)

    mine = lay.spread(chunks(arrived)).reshape(lay.n_d * slots_all, 2 * chunk)
    x_rows, d_rows = mine[:, :chunk], mine[:, chunk:]
    pre_gate = lay.summed(jnp.dot(x_rows, wg, preferred_element_type=F32))
    pre_up = lay.summed(jnp.dot(x_rows, wu, preferred_element_type=F32))
    d_hidden = lay.summed(jnp.dot(d_rows, wd, preferred_element_type=F32))
    sig = jax.nn.sigmoid(pre_gate)
    hidden = (pre_gate * sig * pre_up).astype(BF)
    d_pre_gate = (d_hidden * pre_up * sig * (1.0 + pre_gate * (1.0 - sig))).astype(BF)
    d_pre_up = (d_hidden * pre_gate * sig).astype(BF)
    out_terms = dot(hidden, wd, inner).astype(BF)
    in_terms = (dot(d_pre_gate, wg, inner) + dot(d_pre_up, wu, inner)).astype(BF)
    terms = jnp.concatenate([out_terms, in_terms], axis=1).reshape(lay.n_d, slots_all, 2 * chunk)
    sums = lay.collect(terms)
    if lay.group == 1:
        home = sums[0]
    else:
        home = jnp.moveaxis(sums.reshape(lay.group, slots_all, 2, chunk), 0, 2).reshape(
            slots_all, 2 * half_width
        )
    back = exchanged(home, experts)
    out_rows, in_rows = back[:, :half_width], back[:, half_width:]
    scores = dot(cotangent, out_rows, inner)
    scores = jnp.where(live, scores, 0.0)
    gate_part = jnp.stack(
        [jnp.sum(jnp.where(m, scores, 0.0), axis=1) for m in match], axis=0
    )
    gate_grad = gate_part
    for step in range(1, lay.n_t):
        gate_grad = gate_grad + lax.ppermute(
            gate_part, "tensor", [(i, (i + step) % lay.n_t) for i in range(lay.n_t)]
        )
    gate_grad = gate_grad.T
    layer_out = jnp.dot(weighted, out_rows, preferred_element_type=F32).astype(BF)
    input_grad = jnp.dot(select, in_rows, preferred_element_type=F32).astype(BF)

    partner = [(i, (i + experts // 2) % experts) for i in range(experts)]
    moved = lax.ppermute(arrived, "expert", partner)
    held_rows = jnp.where(my_flag, moved, arrived)
    held_rows = lay.spread(chunks(held_rows)).reshape(lay.n_d * slots_all, 2 * chunk)
    units_all = jnp.concatenate([d_pre_gate, d_pre_up, hidden], axis=1)
    units_own = pick(
        units_all.reshape(lay.n_d, slots_all, 3 * units), lay.d, lay.n_d
    )
    units_moved = lax.ppermute(units_own, "expert", partner)
    units_held = lay.gathered(jnp.where(my_flag, units_moved, units_own)).reshape(
        lay.n_d * slots_all, 3 * units
    )
    hx, hd = held_rows[:, :chunk], held_rows[:, chunk:]
    grads = (
        dot(hx, units_held[:, :units], contract).astype(BF)[None],
        dot(hx, units_held[:, units : 2 * units], contract).astype(BF)[None],
        dot(hd, units_held[:, 2 * units :], contract).astype(BF)[None],
    )
    return (layer_out, input_grad, gate_grad, grads[0], grads[1], grads[2])


def solution(mesh):
    placed = (
        P(("expert", "dp"), "tensor"),
        P(("expert", "dp"), None),
        P(("expert", "dp"), None),
        P(("expert", "dp"), "tensor"),
        P(),
        P(),
        P("expert", "dp", "tensor"),
        P("expert", "dp", "tensor"),
        P("expert", "dp", "tensor"),
    )
    return jax.shard_map(
        on_device,
        mesh=mesh,
        in_specs=placed,
        out_specs=(
            P(("expert", "dp"), "tensor"),
            P(("expert", "dp"), "tensor"),
            P(("expert", "dp"), None),
            P("expert", "dp", "tensor"),
            P("expert", "dp", "tensor"),
            P("expert", "dp", "tensor"),
        ),
        check_vma=False,
    )
```

```python
import jax
import jax.numpy as jnp
from jax import lax
from jax.sharding import PartitionSpec as P

CAP = 9
BF = jnp.bfloat16
F32 = jnp.float32
LANES = 128

contract = (((0,), (0,)), ((), ()))
inner = (((1,), (1,)), ((), ()))


def dot(a, b, dims):
    return lax.dot_general(a, b, dims, preferred_element_type=F32)


def pick(stack, index, count):
    return stack[0] if count == 1 else lax.dynamic_index_in_dim(stack, index, 0, keepdims=False)


class Layout:
    def __init__(self):
        self.n_d = lax.axis_size("dp")
        self.n_t = lax.axis_size("tensor")
        self.group = self.n_d // self.n_t
        self.d = lax.axis_index("dp")
        self.t = lax.axis_index("tensor")
        self.order = (self.d % self.group) * self.n_t + self.t

    def pairs(self, step):
        route = []
        for d in range(self.n_d):
            for t in range(self.n_t):
                half = d // self.group
                data = ((d % self.group) * self.n_t + t + step) % self.n_d
                route.append((data * self.n_t + half, d * self.n_t + t))
        return route

    def canonical(self, blocks):
        if self.group == 1:
            return jnp.stack(blocks)
        whole = jnp.stack(blocks)
        return jnp.take(whole, (jnp.arange(self.n_d) - self.order) % self.n_d, axis=0)

    def spread(self, rows):
        blocks = []
        for step in range(self.n_d):
            target = (self.d - step) % self.n_d
            chunk = pick(rows, target // self.n_t, self.group)
            blocks.append(lax.ppermute(chunk, ("dp", "tensor"), self.pairs(step)))
        return self.canonical(blocks)

    def collect(self, blocks):
        parts = []
        for step in range(self.n_d):
            if self.group == 1:
                block = blocks[step]
            else:
                block = pick(blocks, (self.order + step) % self.n_d, self.n_d)
            route = [(b, a) for a, b in self.pairs(step)]
            got = lax.ppermute(block, ("dp", "tensor"), route)
            got = got.astype(F32)
            source = (self.d - step) % self.n_d
            parts.append(
                jnp.stack([jnp.where(source // self.n_t == c, got, 0.0) for c in range(self.group)])
                if self.group > 1
                else got[None]
            )
        total = parts[0]
        for part in parts[1:]:
            total = total + part
        return total.astype(BF)

    def summed(self, value):
        total = value
        for step in range(1, self.n_d):
            route = [(i, (i + step) % self.n_d) for i in range(self.n_d)]
            other = lax.ppermute(value, "dp", route)
            total = total + other
        return total

    def gathered(self, value):
        if self.n_d == 2:
            other = lax.ppermute(value, "dp", [(0, 1), (1, 0)])
            first = self.d == 0
            return jnp.stack([jnp.where(first, value, other), jnp.where(first, other, value)])
        return lax.all_gather(value, "dp", axis=0)


def exchanged(rows, experts):
    cols = rows.shape[1]
    flat = rows.reshape(experts, CAP * cols // LANES, LANES)
    got = lax.all_to_all(flat, "expert", split_axis=0, concat_axis=0, tiled=True)
    return got.reshape(experts * CAP, cols)


def on_device(tokens, routes, gates, cotangent, placement, swap_flag, w_gate, w_up, w_down):
    experts = lax.axis_size("expert")
    myself = lax.axis_index("expert")
    lay = Layout()
    places = jnp.arange(experts, dtype=jnp.int32)
    my_flag = jnp.sum(jnp.where(places == myself, swap_flag, 0)) == 1
    wg, wu, wd = w_gate[0], w_up[0], w_down[0]
    chunk, units = wg.shape
    tok_count, top_count = routes.shape
    slots_all = experts * CAP
    half_width = tokens.shape[1]

    slot_ids = lax.broadcasted_iota(jnp.int32, (1, slots_all), 1)
    wanted = jnp.repeat(placement, CAP)[None, :]
    match = [routes[:, k : k + 1] == wanted for k in range(top_count)]
    hit = match[0]
    for m in match[1:]:
        hit = hit | m
    weight = jnp.zeros((tok_count, slots_all), F32)
    for k in range(top_count):
        weight = weight + jnp.where(match[k], gates[:, k : k + 1].astype(F32), 0.0)
    row_id = lax.broadcasted_iota(jnp.int32, (tok_count, tok_count), 0)
    col_id = lax.broadcasted_iota(jnp.int32, (tok_count, tok_count), 1)
    before = (col_id < row_id).astype(BF)
    earlier = jnp.dot(before, hit.astype(BF), preferred_element_type=F32)
    live = hit & (earlier == (slot_ids % CAP).astype(F32))
    select = live.astype(BF)
    weighted = jnp.where(live, weight, 0.0).astype(BF)

    outgoing = jnp.concatenate(
        [dot(select, tokens, contract).astype(BF), dot(weighted, cotangent, contract).astype(BF)],
        axis=1,
    )
    arrived = exchanged(outgoing, experts)

    def chunks(rows):
        both = rows.reshape(slots_all, 2, lay.group, chunk)
        if lay.group == 1:
            return rows[None]
        return jnp.moveaxis(both, 2, 0).reshape(lay.group, slots_all, 2 * chunk)

    mine = lay.spread(chunks(arrived)).reshape(lay.n_d * slots_all, 2 * chunk)
    x_rows, d_rows = mine[:, :chunk], mine[:, chunk:]
    pre_gate = lay.summed(jnp.dot(x_rows, wg, preferred_element_type=F32))
    pre_up = lay.summed(jnp.dot(x_rows, wu, preferred_element_type=F32))
    d_hidden = lay.summed(jnp.dot(d_rows, wd, preferred_element_type=F32))
    sig = jax.nn.sigmoid(pre_gate)
    hidden = (pre_gate * sig * pre_up).astype(BF)
    d_pre_gate = (d_hidden * pre_up * sig * (1.0 + pre_gate * (1.0 - sig))).astype(BF)
    d_pre_up = (d_hidden * pre_gate * sig).astype(BF)
    out_terms = dot(hidden, wd, inner).astype(BF)
    in_terms = (dot(d_pre_gate, wg, inner) + dot(d_pre_up, wu, inner)).astype(BF)
    terms = jnp.concatenate([out_terms, in_terms], axis=1).reshape(lay.n_d, slots_all, 2 * chunk)
    sums = lay.collect(terms)
    if lay.group == 1:
        home = sums[0]
    else:
        home = jnp.moveaxis(sums.reshape(lay.group, slots_all, 2, chunk), 0, 2).reshape(
            slots_all, 2 * half_width
        )
    partner = [(i, (i + experts // 2) % experts) for i in range(experts)]
    moved = lax.ppermute(arrived, "expert", partner)
    held_rows = jnp.where(my_flag, moved, arrived)
    back = exchanged(home, experts)
    out_rows, in_rows = back[:, :half_width], back[:, half_width:]
    scores = dot(cotangent, out_rows, inner)
    scores = jnp.where(live, scores, 0.0)
    gate_part = jnp.stack(
        [jnp.sum(jnp.where(m, scores, 0.0), axis=1) for m in match], axis=0
    )
    gate_grad = gate_part
    for step in range(1, lay.n_t):
        gate_grad = gate_grad + lax.ppermute(
            gate_part, "tensor", [(i, (i + step) % lay.n_t) for i in range(lay.n_t)]
        )
    gate_grad = gate_grad.T
    layer_out = jnp.dot(weighted, out_rows, preferred_element_type=F32).astype(BF)
    input_grad = jnp.dot(select, in_rows, preferred_element_type=F32).astype(BF)

    held_rows = lay.spread(chunks(held_rows)).reshape(lay.n_d * slots_all, 2 * chunk)
    units_all = jnp.concatenate([d_pre_gate, d_pre_up, hidden], axis=1)
    units_own = pick(
        units_all.reshape(lay.n_d, slots_all, 3 * units), lay.d, lay.n_d
    )
    units_moved = lax.ppermute(units_own, "expert", partner)
    units_held = lay.gathered(jnp.where(my_flag, units_moved, units_own)).reshape(
        lay.n_d * slots_all, 3 * units
    )
    hx, hd = held_rows[:, :chunk], held_rows[:, chunk:]
    grads = (
        dot(hx, units_held[:, :units], contract).astype(BF)[None],
        dot(hx, units_held[:, units : 2 * units], contract).astype(BF)[None],
        dot(hd, units_held[:, 2 * units :], contract).astype(BF)[None],
    )
    return (layer_out, input_grad, gate_grad, grads[0], grads[1], grads[2])


def solution(mesh):
    placed = (
        P(("expert", "dp"), "tensor"),
        P(("expert", "dp"), None),
        P(("expert", "dp"), None),
        P(("expert", "dp"), "tensor"),
        P(),
        P(),
        P("expert", "dp", "tensor"),
        P("expert", "dp", "tensor"),
        P("expert", "dp", "tensor"),
    )

    return jax.shard_map(
        on_device,
        mesh=mesh,
        in_specs=placed,
        out_specs=(
            P(("expert", "dp"), "tensor"),
            P(("expert", "dp"), "tensor"),
            P(("expert", "dp"), None),
            P("expert", "dp", "tensor"),
            P("expert", "dp", "tensor"),
            P("expert", "dp", "tensor"),
        ),
        check_vma=False,
    )
```

```python
import jax
import jax.numpy as jnp
from jax import lax
from jax.sharding import PartitionSpec as P

CAP = 9
BF = jnp.bfloat16
F32 = jnp.float32
LANES = 128

contract = (((0,), (0,)), ((), ()))
inner = (((1,), (1,)), ((), ()))


def dot(a, b, dims):
    return lax.dot_general(a, b, dims, preferred_element_type=F32)


def pick(stack, index, count):
    return stack[0] if count == 1 else lax.dynamic_index_in_dim(stack, index, 0, keepdims=False)


class Layout:
    def __init__(self):
        self.n_d = lax.axis_size("dp")
        self.n_t = lax.axis_size("tensor")
        self.group = self.n_d // self.n_t
        self.d = lax.axis_index("dp")
        self.t = lax.axis_index("tensor")
        self.order = (self.d % self.group) * self.n_t + self.t

    def pairs(self, step):
        route = []
        for d in range(self.n_d):
            for t in range(self.n_t):
                half = d // self.group
                data = ((d % self.group) * self.n_t + t + step) % self.n_d
                route.append((data * self.n_t + half, d * self.n_t + t))
        return route

    def canonical(self, blocks):
        if self.group == 1:
            return jnp.stack(blocks)
        whole = jnp.stack(blocks)
        return jnp.take(whole, (jnp.arange(self.n_d) - self.order) % self.n_d, axis=0)

    def spread(self, rows):
        blocks = []
        for step in range(self.n_d):
            target = (self.d - step) % self.n_d
            chunk = pick(rows, target // self.n_t, self.group)
            blocks.append(lax.ppermute(chunk, ("dp", "tensor"), self.pairs(step)))
        return self.canonical(blocks)

    def send_back(self, blocks):
        got = []
        for step in range(self.n_d):
            if self.group == 1:
                block = blocks[step]
            else:
                block = pick(blocks, (self.order + step) % self.n_d, self.n_d)
            route = [(b, a) for a, b in self.pairs(step)]
            got.append(lax.ppermute(block, ("dp", "tensor"), route))
        return got

    def add_up(self, got):
        total = None
        for step, block in enumerate(got):
            part = block.astype(F32)[None]
            if self.group > 1:
                place = ((self.d - step) % self.n_d) // self.n_t
                mask = jnp.arange(self.group) == place
                part = jnp.where(mask[:, None, None], part, 0.0)
            total = part if total is None else total + part
        return total.astype(BF)

    def summed(self, value):
        total = value
        for step in range(1, self.n_d):
            route = [(i, (i + step) % self.n_d) for i in range(self.n_d)]
            other = lax.ppermute(value, "dp", route)
            total = total + other
        return total

    def gathered(self, value):
        if self.n_d == 2:
            other = lax.ppermute(value, "dp", [(0, 1), (1, 0)])
            first = self.d == 0
            return jnp.stack([jnp.where(first, value, other), jnp.where(first, other, value)])
        return lax.all_gather(value, "dp", axis=0)


def flat_rows(rows, experts):
    return rows.reshape(experts, CAP * rows.shape[1] // LANES, LANES)


def exchanged(flat):
    got = lax.all_to_all(flat, "expert", split_axis=0, concat_axis=0, tiled=True)
    return got.reshape(flat.shape[0] * CAP, flat.shape[1] * LANES // CAP)


def on_device(tokens, routes, gates, cotangent, placement, swap_flag, w_gate, w_up, w_down):
    experts = lax.axis_size("expert")
    myself = lax.axis_index("expert")
    lay = Layout()
    places = jnp.arange(experts, dtype=jnp.int32)
    my_flag = jnp.sum(jnp.where(places == myself, swap_flag, 0)) == 1
    wg, wu, wd = w_gate[0], w_up[0], w_down[0]
    chunk, units = wg.shape
    tok_count, top_count = routes.shape
    slots_all = experts * CAP
    rows_all = lay.n_d * slots_all
    half_width = tokens.shape[1]

    slot_ids = lax.broadcasted_iota(jnp.int32, (1, slots_all), 1)
    wanted = jnp.repeat(placement, CAP)[None, :]
    match = [routes[:, k : k + 1] == wanted for k in range(top_count)]
    hit = match[0]
    for m in match[1:]:
        hit = hit | m
    weight = jnp.zeros((tok_count, slots_all), F32)
    for k in range(top_count):
        weight = weight + jnp.where(match[k], gates[:, k : k + 1].astype(F32), 0.0)
    row_id = lax.broadcasted_iota(jnp.int32, (tok_count, tok_count), 0)
    col_id = lax.broadcasted_iota(jnp.int32, (tok_count, tok_count), 1)
    before = (col_id < row_id).astype(BF)
    earlier = jnp.dot(before, hit.astype(BF), preferred_element_type=F32)
    live = hit & (earlier == (slot_ids % CAP).astype(F32))
    select = live.astype(BF)
    weighted = jnp.where(live, weight, 0.0).astype(BF)

    outgoing = jnp.concatenate(
        [dot(select, tokens, contract).astype(BF), dot(weighted, cotangent, contract).astype(BF)],
        axis=1,
    )
    outgoing = flat_rows(outgoing, experts)
    arrived = exchanged(outgoing)
    traded = jnp.where(
        (swap_flag == 1)[:, None, None], jnp.roll(outgoing, experts // 2, axis=0), outgoing
    )
    held_rows = exchanged(traded)

    def spread(rows):
        if lay.group == 1:
            pieces = rows[None]
        else:
            pieces = jnp.moveaxis(rows.reshape(slots_all, lay.group, chunk), 1, 0)
        return lay.spread(pieces).reshape(rows_all, chunk)

    def send_back(terms):
        return lay.send_back(terms.reshape(lay.n_d, slots_all, chunk))

    def add_up(got):
        return jnp.moveaxis(lay.add_up(got), 0, 1).reshape(slots_all, half_width)

    x_rows = spread(arrived[:, :half_width])
    d_rows = spread(arrived[:, half_width:])
    pre_gate = lay.summed(jnp.dot(x_rows, wg, preferred_element_type=F32))
    pre_up = lay.summed(jnp.dot(x_rows, wu, preferred_element_type=F32))
    sig = jax.nn.sigmoid(pre_gate)
    hidden = (pre_gate * sig * pre_up).astype(BF)
    pre_gate, pre_up, hidden = lax.optimization_barrier((pre_gate, pre_up, hidden))
    sig = jax.nn.sigmoid(pre_gate)
    out_terms = dot(hidden, wd, inner).astype(BF)
    out_got = send_back(out_terms)
    d_hidden = lay.summed(jnp.dot(d_rows, wd, preferred_element_type=F32))
    d_pre_gate = (d_hidden * pre_up * sig * (1.0 + pre_gate * (1.0 - sig))).astype(BF)
    d_pre_up = (d_hidden * pre_gate * sig).astype(BF)
    in_terms = (dot(d_pre_gate, wg, inner) + dot(d_pre_up, wu, inner)).astype(BF)
    in_got = send_back(in_terms)
    home = jnp.concatenate([add_up(out_got), add_up(in_got)], axis=1)
    back = exchanged(flat_rows(home, experts))
    out_rows, in_rows = back[:, :half_width], back[:, half_width:]
    scores = dot(cotangent, out_rows, inner)
    scores = jnp.where(live, scores, 0.0)
    gate_part = jnp.stack(
        [jnp.sum(jnp.where(m, scores, 0.0), axis=1) for m in match], axis=0
    )
    gate_grad = gate_part
    for step in range(1, lay.n_t):
        other = lax.ppermute(
            gate_part, "tensor", [(i, (i + step) % lay.n_t) for i in range(lay.n_t)]
        )
        gate_grad = gate_grad + other
    gate_grad = gate_grad.T
    layer_out = jnp.dot(weighted, out_rows, preferred_element_type=F32).astype(BF)
    input_grad = jnp.dot(select, in_rows, preferred_element_type=F32).astype(BF)

    units_all = jnp.concatenate([d_pre_gate, d_pre_up, hidden], axis=1)
    units_own = pick(units_all.reshape(lay.n_d, slots_all, 3 * units), lay.d, lay.n_d)
    partner = [(i, (i + experts // 2) % experts) for i in range(experts)]
    units_moved = lax.ppermute(units_own, "expert", partner)
    units_held = jnp.where(my_flag, units_moved, units_own)
    units_held = lay.gathered(units_held).reshape(rows_all, 3 * units)
    hx = spread(held_rows[:, :half_width])
    hd = spread(held_rows[:, half_width:])
    grads = (
        dot(hx, units_held[:, :units], contract).astype(BF)[None],
        dot(hx, units_held[:, units : 2 * units], contract).astype(BF)[None],
        dot(hd, units_held[:, 2 * units :], contract).astype(BF)[None],
    )
    return (layer_out, input_grad, gate_grad, grads[0], grads[1], grads[2])


def solution(mesh):
    placed = (
        P(("expert", "dp"), "tensor"),
        P(("expert", "dp"), None),
        P(("expert", "dp"), None),
        P(("expert", "dp"), "tensor"),
        P(),
        P(),
        P("expert", "dp", "tensor"),
        P("expert", "dp", "tensor"),
        P("expert", "dp", "tensor"),
    )


    return jax.shard_map(
        on_device,
        mesh=mesh,
        in_specs=placed,
        out_specs=(
            P(("expert", "dp"), "tensor"),
            P(("expert", "dp"), "tensor"),
            P(("expert", "dp"), None),
            P("expert", "dp", "tensor"),
            P("expert", "dp", "tensor"),
            P("expert", "dp", "tensor"),
        ),
        check_vma=False,
    )
```

```python
import jax
import jax.numpy as jnp
from jax import lax
from jax.experimental import pallas as pl
from jax.experimental.pallas import tpu as pltpu
from jax.sharding import PartitionSpec as P

CAP = 9
BF = jnp.bfloat16
F32 = jnp.float32
LANES = 128

ROWS_AT_ONCE = 320
contract = (((0,), (0,)), ((), ()))
inner = (((1,), (1,)), ((), ()))


def dot(a, b, dims):
    return lax.dot_general(a, b, dims, preferred_element_type=F32)


def pick(stack, index, count):
    return stack[0] if count == 1 else lax.dynamic_index_in_dim(stack, index, 0, keepdims=False)


class Layout:
    def __init__(self):
        self.n_d = lax.axis_size("dp")
        self.n_t = lax.axis_size("tensor")
        self.group = self.n_d // self.n_t
        self.d = lax.axis_index("dp")
        self.t = lax.axis_index("tensor")
        self.order = (self.d % self.group) * self.n_t + self.t

    def pairs(self, step):
        route = []
        for d in range(self.n_d):
            for t in range(self.n_t):
                half = d // self.group
                data = ((d % self.group) * self.n_t + t + step) % self.n_d
                route.append((data * self.n_t + half, d * self.n_t + t))
        return route

    def canonical(self, blocks):
        if self.group == 1:
            return blocks
        whole = jnp.stack(blocks)
        whole = jnp.take(whole, (jnp.arange(self.n_d) - self.order) % self.n_d, axis=0)
        return [whole[i] for i in range(self.n_d)]

    def spread(self, rows):
        blocks = []
        for step in range(self.n_d):
            target = (self.d - step) % self.n_d
            chunk = pick(rows, target // self.n_t, self.group)
            blocks.append(lax.ppermute(chunk, ("dp", "tensor"), self.pairs(step)))
        return self.canonical(blocks)

    def send_back(self, blocks):
        got = []
        for step in range(self.n_d):
            if self.group == 1:
                block = blocks[step]
            else:
                block = pick(jnp.stack(blocks), (self.order + step) % self.n_d, self.n_d)
            route = [(b, a) for a, b in self.pairs(step)]
            got.append(lax.ppermute(block, ("dp", "tensor"), route))
        return got

    def add_up(self, got):
        total = None
        for step, block in enumerate(got):
            part = block.astype(F32)[None]
            if self.group > 1:
                place = ((self.d - step) % self.n_d) // self.n_t
                mask = jnp.arange(self.group) == place
                part = jnp.where(mask[:, None, None], part, 0.0)
            total = part if total is None else total + part
        return total.astype(BF)

    def others(self, value):
        got = []
        for step in range(1, self.n_d):
            route = [(i, (i + step) % self.n_d) for i in range(self.n_d)]
            got.append(lax.ppermute(value, "dp", route))
        return got

    def gathered(self, value):
        if self.n_d == 2:
            other = lax.ppermute(value, "dp", [(0, 1), (1, 0)])
            first = self.d == 0
            return jnp.concatenate([jnp.where(first, value, other), jnp.where(first, other, value)])
        return lax.all_gather(value, "dp", axis=0, tiled=True)


def exchanged(rows, experts):
    cols = rows.shape[1]
    flat = rows.reshape(experts, CAP * cols // LANES, LANES)
    got = lax.all_to_all(flat, "expert", split_axis=0, concat_axis=0, tiled=True)
    return got.reshape(experts * CAP, cols)


def call(kernel, outs, args, room, smem=0, flops=0):
    vmem = pl.BlockSpec(memory_space=pltpu.VMEM)
    moved = sum(a.size * a.dtype.itemsize for a in args) + sum(
        o.size * o.dtype.itemsize for o in outs
    )
    return pl.pallas_call(
        kernel,
        out_shape=outs,
        in_specs=[pl.BlockSpec(memory_space=pltpu.SMEM)] * smem + [vmem] * (len(args) - smem),
        out_specs=[vmem] * len(outs),
        compiler_params=pltpu.CompilerParams(vmem_limit_bytes=room),
        cost_estimate=pl.CostEstimate(flops=flops, bytes_accessed=moved, transcendentals=0),
    )(*args)


def room_for(*arrays):
    return (6 << 20) + 3 * sum(a.size * a.dtype.itemsize for a in arrays) // 2


def shape(dims, dtype):
    return jax.ShapeDtypeStruct(dims, dtype)


def wanted_column(placement, slots):
    row = lax.broadcasted_iota(jnp.int32, (slots, 1), 0)
    wanted = jnp.zeros((slots, 1), jnp.int32)
    base = jnp.zeros((slots, 1), jnp.int32)
    for e in range(slots // CAP):
        inside = row >= e * CAP
        wanted = jnp.where(inside, placement[e], wanted)
        base = jnp.where(inside, e * CAP, base)
    return wanted, row - base


def head_kernel(placement, routes, gates, tokens, cot, rows, select, weighted):
    slots, tok_count = select.shape
    top_count = routes.shape[0]
    half = tokens.shape[1]
    wanted, slot = wanted_column(placement, slots)
    hit = jnp.zeros((slots, tok_count), F32)
    weight = jnp.zeros((slots, tok_count), F32)
    for k in range(top_count):
        match = routes[k : k + 1, :] == wanted
        hit = jnp.where(match, 1.0, hit)
        weight = jnp.where(match, gates[k : k + 1, :].astype(F32), weight)
    row_id = lax.broadcasted_iota(jnp.int32, (tok_count, tok_count), 0)
    col_id = lax.broadcasted_iota(jnp.int32, (tok_count, tok_count), 1)
    before = jnp.where(row_id < col_id, 1.0, 0.0).astype(BF)
    earlier = jnp.dot(hit.astype(BF), before, preferred_element_type=F32)
    live = (hit > 0.0) & (earlier == slot.astype(F32))
    chosen = jnp.where(live, 1.0, 0.0).astype(BF)
    scaled = jnp.where(live, weight, 0.0).astype(BF)
    select[...] = chosen
    weighted[...] = scaled
    rows[:, :half] = jnp.dot(chosen, tokens[...], preferred_element_type=F32).astype(BF)
    rows[:, half:] = jnp.dot(scaled, cot[...], preferred_element_type=F32).astype(BF)


def first_kernel(xd, wg, wu, wd, terms):
    chunk, units = wg.shape
    x, d = xd[:, :chunk], xd[:, chunk:]
    terms[:, :units] = jnp.dot(x, wg[...], preferred_element_type=F32)
    terms[:, units : 2 * units] = jnp.dot(x, wu[...], preferred_element_type=F32)
    terms[:, 2 * units :] = jnp.dot(d, wd[...], preferred_element_type=F32)


def middle_kernel(count, *refs):
    parts, (wg, wu, wd) = refs[:count], refs[count : count + 3]
    units_out, results = refs[count + 3], refs[count + 4 :]
    chunk, units = wg.shape
    blocks, rows = units_out.shape[:2]
    at_once = blocks if blocks * rows <= ROWS_AT_ONCE else 1
    for first in range(0, blocks, at_once):
        span = pl.ds(first * rows, at_once * rows)

        def total(which):
            cols = pl.ds(which * units, units)
            value = parts[0][span, cols]
            for part in parts[1:]:
                value = value + part[span, cols]
            return value

        gate, up, d_hidden = total(0), total(1), total(2)
        sig = jax.nn.sigmoid(gate)
        hidden = (gate * sig * up).astype(BF)
        d_gate = (d_hidden * up * sig * (1.0 + gate * (1.0 - sig))).astype(BF)
        d_up = (d_hidden * gate * sig).astype(BF)
        out = dot(hidden, wd[...], inner)
        back = dot(d_gate, wg[...], inner) + dot(d_up, wu[...], inner)
        for j in range(at_once):
            part = slice(j * rows, (j + 1) * rows)
            results[first + j][:, :chunk] = out[part].astype(BF)
            results[first + j][:, chunk:] = back[part].astype(BF)
            units_out[first + j, :, :units] = d_gate.astype(F32)[part].astype(BF)
            units_out[first + j, :, units : 2 * units] = d_up.astype(F32)[part].astype(BF)
            units_out[first + j, :, 2 * units :] = hidden.astype(F32)[part].astype(BF)


def gate_kernel(placement, routes, select, cot, back, gate_part):
    slots = select.shape[0]
    half = cot.shape[1]
    wanted, _ = wanted_column(placement, slots)
    scores = dot(back[:, :half], cot[...], inner)
    scores = jnp.where(select[...].astype(F32) > 0.0, scores, 0.0)
    for k in range(routes.shape[0]):
        match = routes[k : k + 1, :] == wanted
        gate_part[k : k + 1, :] = jnp.sum(
            jnp.where(match, scores, 0.0), axis=0, keepdims=True
        )


def combine_kernel(select, weighted, back, layer_out, input_grad):
    half = layer_out.shape[1]
    layer_out[...] = dot(weighted[...], back[:, :half], contract).astype(BF)
    input_grad[...] = dot(select[...], back[:, half:], contract).astype(BF)


def grads_kernel(x, d, units_ref, g_gate, g_up, g_down):
    units = g_gate.shape[1]
    both = dot(x[...], units_ref[:, : 2 * units], contract).astype(BF)
    g_gate[...] = both[:, :units]
    g_up[...] = both[:, units:]
    g_down[...] = dot(d[...], units_ref[:, 2 * units :], contract).astype(BF)


def weight_grads(held, units_held, chunk, units):
    rows = held.shape[0]
    block = 256 if chunk % 256 == 0 else LANES
    steps = chunk // block
    out = shape((chunk, units), BF)
    spec = pl.BlockSpec((block, units), lambda i: (i, 0))
    return pl.pallas_call(
        grads_kernel,
        grid=(steps,),
        out_shape=[out] * 3,
        in_specs=[
            pl.BlockSpec((rows, block), lambda i: (0, i)),
            pl.BlockSpec((rows, block), lambda i: (0, i + steps)),
            pl.BlockSpec((rows, 3 * units), lambda i: (0, 0)),
        ],
        out_specs=[spec] * 3,
        compiler_params=pltpu.CompilerParams(
            vmem_limit_bytes=(6 << 20) + 3 * rows * 2 * (3 * units + 2 * block)
        ),
        cost_estimate=pl.CostEstimate(
            flops=6 * rows * chunk * units, bytes_accessed=6 * chunk * units, transcendentals=0
        ),
        name="weight_grads",
    )(held, held, units_held)


def on_device(tokens, routes, gates, cotangent, placement, swap_flag, w_gate, w_up, w_down):
    experts = lax.axis_size("expert")
    myself = lax.axis_index("expert")
    lay = Layout()
    places = jnp.arange(experts, dtype=jnp.int32)
    my_flag = jnp.sum(jnp.where(places == myself, swap_flag, 0)) == 1
    wg, wu, wd = w_gate[0], w_up[0], w_down[0]
    chunk, units = wg.shape
    tok_count, top_count = routes.shape
    slots_all = experts * CAP
    rows_all = lay.n_d * slots_all
    half_width = tokens.shape[1]
    routes_t, gates_t = routes.T, gates.T

    outs = [
        shape((slots_all, 2 * half_width), BF),
        shape((slots_all, tok_count), BF),
        shape((slots_all, tok_count), BF),
    ]
    outgoing, select, weighted = call(
        head_kernel,
        outs,
        (placement, routes_t, gates_t, tokens, cotangent),
        room_for(tokens, cotangent, *outs),
        smem=1,
    )
    arrived = exchanged(outgoing, experts)

    def spread(rows):
        if lay.group == 1:
            pieces = rows[None]
        else:
            both = rows.reshape(slots_all, 2, lay.group, chunk)
            pieces = jnp.moveaxis(both, 2, 0).reshape(lay.group, slots_all, 2 * chunk)
        return jnp.concatenate(lay.spread(pieces), axis=0)

    xd = spread(arrived)
    partial_sums = shape((rows_all, 3 * units), F32)
    (own_terms,) = call(
        first_kernel,
        [partial_sums],
        (xd, wg, wu, wd),
        room_for(xd, wg, wu, wd, partial_sums),
        flops=6 * rows_all * chunk * units,
    )
    parts = [own_terms, *lay.others(own_terms)]
    outs = [shape((lay.n_d, slots_all, 3 * units), BF)]
    outs += [shape((slots_all, 2 * chunk), BF)] * lay.n_d
    units_all, *results = call(
        lambda *refs: middle_kernel(lay.n_d, *refs),
        outs,
        (*parts, wg, wu, wd),
        room_for(*parts, wg, wu, wd, *outs),
        flops=6 * rows_all * chunk * units,
    )
    sums = lay.add_up(lay.send_back(results))
    if lay.group == 1:
        home = sums[0]
    else:
        home = jnp.moveaxis(sums.reshape(lay.group, slots_all, 2, chunk), 0, 2)
        home = home.reshape(slots_all, 2 * half_width)
    back = exchanged(home, experts)

    gate_shape = shape((top_count, tok_count), F32)
    (gate_part,) = call(
        gate_kernel,
        [gate_shape],
        (placement, routes_t, select, cotangent, back),
        room_for(cotangent, back),
        smem=1,
    )
    gate_grad = gate_part
    for step in range(1, lay.n_t):
        other = lax.ppermute(
            gate_part, "tensor", [(i, (i + step) % lay.n_t) for i in range(lay.n_t)]
        )
        gate_grad = gate_grad + other
    gate_grad = gate_grad.T
    outs = [shape(tokens.shape, BF)] * 2
    layer_out, input_grad = call(
        combine_kernel, outs, (select, weighted, back), room_for(back, *outs)
    )

    partner = [(i, (i + experts // 2) % experts) for i in range(experts)]
    moved = lax.ppermute(arrived, "expert", partner)
    held = spread(jnp.where(my_flag, moved, arrived))
    units_own = pick(units_all, lay.d, lay.n_d)
    units_moved = lax.ppermute(units_own, "expert", partner)
    units_held = jnp.where(my_flag, units_moved, units_own)
    units_held = lay.gathered(units_held)
    grads = weight_grads(held, units_held, chunk, units)
    return (layer_out, input_grad, gate_grad, grads[0][None], grads[1][None], grads[2][None])


def solution(mesh):
    placed = (
        P(("expert", "dp"), "tensor"),
        P(("expert", "dp"), None),
        P(("expert", "dp"), None),
        P(("expert", "dp"), "tensor"),
        P(),
        P(),
        P("expert", "dp", "tensor"),
        P("expert", "dp", "tensor"),
        P("expert", "dp", "tensor"),
    )


    return jax.shard_map(
        on_device,
        mesh=mesh,
        in_specs=placed,
        out_specs=(
            P(("expert", "dp"), "tensor"),
            P(("expert", "dp"), "tensor"),
            P(("expert", "dp"), None),
            P("expert", "dp", "tensor"),
            P("expert", "dp", "tensor"),
            P("expert", "dp", "tensor"),
        ),
        check_vma=False,
    )
```

```python
import jax
import jax.numpy as jnp
from jax import lax
from jax.experimental import pallas as pl
from jax.experimental.pallas import tpu as pltpu
from jax.sharding import PartitionSpec as P

CAP = 9
BF = jnp.bfloat16
F32 = jnp.float32
LANES = 128

contract = (((0,), (0,)), ((), ()))
inner = (((1,), (1,)), ((), ()))


def dot(a, b, dims):
    return lax.dot_general(a, b, dims, preferred_element_type=F32)


def pick(stack, index, count):
    return stack[0] if count == 1 else lax.dynamic_index_in_dim(stack, index, 0, keepdims=False)


class Layout:
    def __init__(self):
        self.n_d = lax.axis_size("dp")
        self.n_t = lax.axis_size("tensor")
        self.group = self.n_d // self.n_t
        self.d = lax.axis_index("dp")
        self.t = lax.axis_index("tensor")
        self.order = (self.d % self.group) * self.n_t + self.t

    def pairs(self, step):
        route = []
        for d in range(self.n_d):
            for t in range(self.n_t):
                half = d // self.group
                data = ((d % self.group) * self.n_t + t + step) % self.n_d
                route.append((data * self.n_t + half, d * self.n_t + t))
        return route

    def canonical(self, blocks):
        if self.group == 1:
            return blocks
        whole = jnp.stack(blocks)
        whole = jnp.take(whole, (jnp.arange(self.n_d) - self.order) % self.n_d, axis=0)
        return [whole[i] for i in range(self.n_d)]

    def spread(self, rows):
        blocks = []
        for step in range(self.n_d):
            target = (self.d - step) % self.n_d
            chunk = pick(rows, target // self.n_t, self.group)
            blocks.append(lax.ppermute(chunk, ("dp", "tensor"), self.pairs(step)))
        return self.canonical(blocks)

    def flipped(self, values):
        got = []
        for step in range(1, self.n_t):
            route = [(i, (i + step) % self.n_t) for i in range(self.n_t)]
            got.append(lax.ppermute(values[step - 1], "tensor", route))
        return got

    def others(self, value):
        got = []
        for step in range(1, self.n_d):
            route = [(i, (i + step) % self.n_d) for i in range(self.n_d)]
            got.append(lax.ppermute(value, "dp", route))
        return got

    def gathered(self, value):
        if self.n_d == 2 and self.group == 1:
            other = lax.ppermute(value, "dp", [(0, 1), (1, 0)])
            first = self.d == self.order
            return jnp.concatenate([jnp.where(first, value, other), jnp.where(first, other, value)])
        return lax.all_gather(value, "dp", axis=0, tiled=True)


def exchanged(rows, experts):
    cols = rows.shape[1]
    flat = rows.reshape(experts, CAP * cols // LANES, LANES)
    got = lax.all_to_all(flat, "expert", split_axis=0, concat_axis=0, tiled=True)
    return got.reshape(experts * CAP, cols)


def call(kernel, outs, args, room, smem=0, hbm=0, scratch=(), flops=0):
    space = pl.ANY if scratch else pltpu.VMEM
    moved = sum(a.size * a.dtype.itemsize for a in args) + sum(
        o.size * o.dtype.itemsize for o in outs
    )
    return pl.pallas_call(
        kernel,
        out_shape=outs,
        in_specs=[pl.BlockSpec(memory_space=pltpu.SMEM)] * smem
        + [pl.BlockSpec(memory_space=pltpu.HBM)] * hbm
        + [pl.BlockSpec(memory_space=space)] * (len(args) - smem - hbm),
        out_specs=[pl.BlockSpec(memory_space=pltpu.VMEM)] * len(outs),
        scratch_shapes=scratch,
        compiler_params=pltpu.CompilerParams(vmem_limit_bytes=None if scratch else room),
        cost_estimate=pl.CostEstimate(flops=flops, bytes_accessed=moved, transcendentals=0),
    )(*args)


def room_for(*arrays):
    return (6 << 20) + 3 * sum(a.size * a.dtype.itemsize for a in arrays) // 2


def shape(dims, dtype):
    return jax.ShapeDtypeStruct(dims, dtype)


def wanted_column(placement, slots):
    row = lax.broadcasted_iota(jnp.int32, (slots, 1), 0)
    wanted = jnp.zeros((slots, 1), jnp.int32)
    base = jnp.zeros((slots, 1), jnp.int32)
    for e in range(slots // CAP):
        inside = row >= e * CAP
        wanted = jnp.where(inside, placement[e], wanted)
        base = jnp.where(inside, e * CAP, base)
    return wanted, row - base


def fetch(pairs, sems):
    copies = [pltpu.make_async_copy(x, y, sems.at[i]) for i, (x, y) in enumerate(pairs)]
    for copy in copies:
        copy.start()
    return copies


def head_kernel(*refs):
    given, (rows, select, weighted), kept = refs[:5], refs[5:8], refs[8:13]
    copies = fetch(zip(given, kept), refs[13])
    placement, routes, gates, tokens, cot = kept
    for copy in copies[:3]:
        copy.wait()
    slots, tok_count = select.shape
    top_count = routes.shape[0]
    half = tokens.shape[1]
    wanted, slot = wanted_column(placement, slots)
    hit = jnp.zeros((slots, tok_count), F32)
    weight = jnp.zeros((slots, tok_count), F32)
    for k in range(top_count):
        match = routes[k : k + 1, :] == wanted
        hit = jnp.where(match, 1.0, hit)
        weight = jnp.where(match, gates[k : k + 1, :].astype(F32), weight)
    row_id = lax.broadcasted_iota(jnp.int32, (tok_count, tok_count), 0)
    col_id = lax.broadcasted_iota(jnp.int32, (tok_count, tok_count), 1)
    before = jnp.where(row_id < col_id, 1.0, 0.0).astype(BF)
    earlier = jnp.dot(hit.astype(BF), before, preferred_element_type=F32)
    live = (hit > 0.0) & (earlier == slot.astype(F32))
    chosen = jnp.where(live, 1.0, 0.0).astype(BF)
    scaled = jnp.where(live, weight, 0.0).astype(BF)
    select[...] = chosen
    weighted[...] = scaled
    copies[3].wait()
    rows[:, :half] = jnp.dot(chosen, tokens[...], preferred_element_type=F32).astype(BF)
    copies[4].wait()
    rows[:, half:] = jnp.dot(scaled, cot[...], preferred_element_type=F32).astype(BF)


def expert_kernel(n_d, n_t, *refs):
    shards, rows_in = refs[: 3 * n_d], refs[3 * n_d : 3 * n_d + n_t]
    refs = refs[3 * n_d + n_t :]
    units_out, terms, (w, x, w_sems, x_sems) = refs[0], refs[1 : 1 + n_t], refs[1 + n_t :]
    d, t = lax.axis_index("dp"), lax.axis_index("tensor")
    chunk, units = w.shape[2:]
    half = x.shape[2] // 2
    group = n_d // n_t
    x_copies = fetch(
        [(rows_in[s], x.at[lax.rem(t - s + n_t, n_t)]) for s in range(n_t)], x_sems
    )
    w_copies = fetch(
        [
            (shards[which * n_d + s], w.at[which, lax.rem(d - s + n_d, n_d)])
            for which in range(3)
            for s in range(n_d)
        ],
        w_sems,
    )
    for copy in x_copies:
        copy.wait()

    def product(which, offset):
        for copy in w_copies[which * n_d : (which + 1) * n_d]:
            copy.wait()
        value = None
        for s in range(n_d):
            cols = pl.ds(offset + (s % group) * chunk, chunk)
            part = jnp.dot(x[s // group, :, cols], w[which, s], preferred_element_type=F32)
            value = part if value is None else value + part
        return value

    gate, up = product(0, 0), product(1, 0)
    sig = jax.nn.sigmoid(gate)
    hidden = (gate * sig * up).astype(BF)
    d_hidden = product(2, half)
    d_gate = (d_hidden * up * sig * (1.0 + gate * (1.0 - sig))).astype(BF)
    d_up = (d_hidden * gate * sig).astype(BF)
    units_out[:, :units] = d_gate
    units_out[:, units : 2 * units] = d_up
    units_out[:, 2 * units :] = hidden
    for s in range(n_d):
        out = dot(hidden, w[2, s], inner).astype(BF)
        back = (dot(d_gate, w[0, s], inner) + dot(d_up, w[1, s], inner)).astype(BF)
        col = (s % group) * chunk
        step = lax.rem(s // group - t + n_t, n_t)
        for k in range(n_t):

            @pl.when(step == k)
            def _():
                terms[k][:, col : col + chunk] = out
                terms[k][:, half + col : half + col + chunk] = back


def gate_kernel(placement, routes, select, cot, back, gate_part):
    slots = select.shape[0]
    half = cot.shape[1]
    wanted, _ = wanted_column(placement, slots)
    scores = dot(back[:, :half], cot[...], inner)
    scores = jnp.where(select[...].astype(F32) > 0.0, scores, 0.0)
    for k in range(routes.shape[0]):
        match = routes[k : k + 1, :] == wanted
        gate_part[k : k + 1, :] = jnp.sum(
            jnp.where(match, scores, 0.0), axis=0, keepdims=True
        )


def combine_kernel(select, weighted, back, layer_out, input_grad):
    half = layer_out.shape[1]
    layer_out[...] = dot(weighted[...], back[:, :half], contract).astype(BF)
    input_grad[...] = dot(select[...], back[:, half:], contract).astype(BF)


def grads_kernel(x, d, units_ref, g_gate, g_up, g_down):
    units = g_gate.shape[1]
    both = dot(x[...], units_ref[:, : 2 * units], contract).astype(BF)
    g_gate[...] = both[:, :units]
    g_up[...] = both[:, units:]
    g_down[...] = dot(d[...], units_ref[:, 2 * units :], contract).astype(BF)


def weight_grads(held, units_held, chunk, units):
    rows = held.shape[0]
    block = next(b for b in (896, 512, 256, LANES) if chunk % b == 0)
    steps = chunk // block
    out = shape((chunk, units), BF)
    spec = pl.BlockSpec((block, units), lambda i: (i, 0))
    return pl.pallas_call(
        grads_kernel,
        grid=(steps,),
        out_shape=[out] * 3,
        in_specs=[
            pl.BlockSpec((rows, block), lambda i: (0, i)),
            pl.BlockSpec((rows, block), lambda i: (0, i + steps)),
            pl.BlockSpec((rows, 3 * units), lambda i: (0, 0)),
        ],
        out_specs=[spec] * 3,
        compiler_params=pltpu.CompilerParams(
            vmem_limit_bytes=(6 << 20) + 3 * rows * 2 * (3 * units + 2 * block)
        ),
        cost_estimate=pl.CostEstimate(
            flops=6 * rows * chunk * units, bytes_accessed=6 * chunk * units, transcendentals=0
        ),
        name="weight_grads",
    )(held, held, units_held)


def on_device(tokens, routes, gates, cotangent, placement, swap_flag, w_gate, w_up, w_down):
    experts = lax.axis_size("expert")
    myself = lax.axis_index("expert")
    lay = Layout()
    places = jnp.arange(experts, dtype=jnp.int32)
    my_flag = jnp.sum(jnp.where(places == myself, swap_flag, 0)) == 1
    wg, wu, wd = w_gate[0], w_up[0], w_down[0]
    chunk, units = wg.shape
    tok_count, top_count = routes.shape
    slots_all = experts * CAP
    half_width = tokens.shape[1]
    routes_t, gates_t = routes.T, gates.T

    outs = [
        shape((slots_all, 2 * half_width), BF),
        shape((slots_all, tok_count), BF),
        shape((slots_all, tok_count), BF),
    ]
    given = (placement, routes_t, gates_t, tokens, cotangent)
    outgoing, select, weighted = call(
        head_kernel,
        outs,
        given,
        room_for(tokens, cotangent, *outs),
        hbm=len(given),
        scratch=[
            pltpu.SMEM(placement.shape, jnp.int32),
            *(pltpu.VMEM(x.shape, x.dtype) for x in given[1:]),
            pltpu.SemaphoreType.DMA((len(given),)),
        ],
    )
    arrived = exchanged(outgoing, experts)

    others = lay.flipped([arrived] * (lay.n_t - 1))
    shards = []
    for own in (wg, wu, wd):
        shards += [own, *lay.others(own)]
    weights_room = shape((3, lay.n_d, chunk, units), BF)
    rows_room = shape((lay.n_t, slots_all, 2 * half_width), BF)
    outs = [shape((slots_all, 3 * units), BF)]
    outs += [shape((slots_all, 2 * half_width), BF)] * lay.n_t
    units_own, *terms = call(
        lambda *refs: expert_kernel(lay.n_d, lay.n_t, *refs),
        outs,
        (*shards, arrived, *others),
        room_for(weights_room, rows_room, *outs),
        hbm=len(shards),
        scratch=[
            pltpu.VMEM(weights_room.shape, BF),
            pltpu.VMEM(rows_room.shape, BF),
            pltpu.SemaphoreType.DMA((3 * lay.n_d,)),
            pltpu.SemaphoreType.DMA((lay.n_t,)),
        ],
        flops=12 * slots_all * lay.n_d * chunk * units,
    )
    home = terms[0].astype(F32)
    for got in lay.flipped(terms[1:]):
        home = home + got.astype(F32)
    back = exchanged(home.astype(BF), experts)

    gate_shape = shape((top_count, tok_count), F32)
    (gate_part,) = call(
        gate_kernel,
        [gate_shape],
        (placement, routes_t, select, cotangent, back),
        room_for(cotangent, back),
        smem=1,
    )
    gate_grad = gate_part
    for step in range(1, lay.n_t):
        other = lax.ppermute(
            gate_part, "tensor", [(i, (i + step) % lay.n_t) for i in range(lay.n_t)]
        )
        gate_grad = gate_grad + other
    gate_grad = gate_grad.T
    outs = [shape(tokens.shape, BF)] * 2
    layer_out, input_grad = call(
        combine_kernel, outs, (select, weighted, back), room_for(back, *outs)
    )

    partner = [(i, (i + experts // 2) % experts) for i in range(experts)]
    moved = lax.ppermute(arrived, "expert", partner)
    held = jnp.where(my_flag, moved, arrived)
    if lay.group == 1:
        pieces = held[None]
    else:
        pieces = jnp.moveaxis(held.reshape(slots_all, 2, lay.group, chunk), 2, 0)
        pieces = pieces.reshape(lay.group, slots_all, 2 * chunk)
    held = jnp.concatenate(lay.spread(pieces), axis=0)
    units_moved = lax.ppermute(units_own, "expert", partner)
    units_held = jnp.where(my_flag, units_moved, units_own)
    units_held = lay.gathered(units_held)
    grads = weight_grads(held, units_held, chunk, units)
    return (layer_out, input_grad, gate_grad, grads[0][None], grads[1][None], grads[2][None])


def solution(mesh):
    placed = (
        P(("expert", "dp"), "tensor"),
        P(("expert", "dp"), None),
        P(("expert", "dp"), None),
        P(("expert", "dp"), "tensor"),
        P(),
        P(),
        P("expert", "dp", "tensor"),
        P("expert", "dp", "tensor"),
        P("expert", "dp", "tensor"),
    )


    return jax.shard_map(
        on_device,
        mesh=mesh,
        in_specs=placed,
        out_specs=(
            P(("expert", "dp"), "tensor"),
            P(("expert", "dp"), "tensor"),
            P(("expert", "dp"), None),
            P("expert", "dp", "tensor"),
            P("expert", "dp", "tensor"),
            P("expert", "dp", "tensor"),
        ),
        check_vma=False,
    )
```

```python
import jax
import jax.numpy as jnp
from jax import lax
from jax.experimental import pallas as pl
from jax.experimental.pallas import tpu as pltpu
from jax.sharding import PartitionSpec as P

CAP = 9
BF = jnp.bfloat16
F32 = jnp.float32
LANES = 128

contract = (((0,), (0,)), ((), ()))
inner = (((1,), (1,)), ((), ()))


def dot(a, b, dims):
    return lax.dot_general(a, b, dims, preferred_element_type=F32)


def pick(stack, index, count):
    return stack[0] if count == 1 else lax.dynamic_index_in_dim(stack, index, 0, keepdims=False)


class Layout:
    def __init__(self):
        self.n_d = lax.axis_size("dp")
        self.n_t = lax.axis_size("tensor")
        self.group = self.n_d // self.n_t
        self.d = lax.axis_index("dp")
        self.t = lax.axis_index("tensor")
        self.order = (self.d % self.group) * self.n_t + self.t

    def pairs(self, step):
        route = []
        for d in range(self.n_d):
            for t in range(self.n_t):
                half = d // self.group
                data = ((d % self.group) * self.n_t + t + step) % self.n_d
                route.append((data * self.n_t + half, d * self.n_t + t))
        return route

    def canonical(self, blocks):
        if self.group == 1:
            return blocks
        whole = jnp.stack(blocks)
        whole = jnp.take(whole, (jnp.arange(self.n_d) - self.order) % self.n_d, axis=0)
        return [whole[i] for i in range(self.n_d)]

    def spread(self, rows):
        blocks = []
        for step in range(self.n_d):
            target = (self.d - step) % self.n_d
            chunk = pick(rows, target // self.n_t, self.group)
            blocks.append(lax.ppermute(chunk, ("dp", "tensor"), self.pairs(step)))
        return self.canonical(blocks)

    def flipped(self, values):
        got = []
        for step in range(1, self.n_t):
            route = [(i, (i + step) % self.n_t) for i in range(self.n_t)]
            got.append(lax.ppermute(values[step - 1], "tensor", route))
        return got

    def others(self, value):
        got = []
        for step in range(1, self.n_d):
            route = [(i, (i + step) % self.n_d) for i in range(self.n_d)]
            got.append(lax.ppermute(value, "dp", route))
        return got

    def gathered(self, value):
        if self.n_d == 2 and self.group == 1:
            other = lax.ppermute(value, "dp", [(0, 1), (1, 0)])
            first = self.d == self.order
            return jnp.concatenate([jnp.where(first, value, other), jnp.where(first, other, value)])
        return lax.all_gather(value, "dp", axis=0, tiled=True)


def exchanged(rows, experts):
    cols = rows.shape[1]
    flat = rows.reshape(experts, CAP * cols // LANES, LANES)
    got = lax.all_to_all(flat, "expert", split_axis=0, concat_axis=0, tiled=True)
    return got.reshape(experts * CAP, cols)


def call(kernel, outs, args, room, smem=0, far=0, scratch=(), flops=0):
    moved = sum(a.size * a.dtype.itemsize for a in args) + sum(
        o.size * o.dtype.itemsize for o in outs
    )
    return pl.pallas_call(
        kernel,
        out_shape=outs,
        in_specs=[pl.BlockSpec(memory_space=pltpu.SMEM)] * smem
        + [pl.BlockSpec(memory_space=pl.ANY)] * far
        + [pl.BlockSpec(memory_space=pltpu.VMEM)] * (len(args) - smem - far),
        out_specs=[pl.BlockSpec(memory_space=pltpu.VMEM)] * len(outs),
        scratch_shapes=scratch,
        compiler_params=pltpu.CompilerParams(vmem_limit_bytes=room),
        cost_estimate=pl.CostEstimate(flops=flops, bytes_accessed=moved, transcendentals=0),
    )(*args)


def room_for(*arrays):
    return (6 << 20) + 3 * sum(a.size * a.dtype.itemsize for a in arrays) // 2


def shape(dims, dtype):
    return jax.ShapeDtypeStruct(dims, dtype)


def wanted_column(placement, slots):
    row = lax.broadcasted_iota(jnp.int32, (slots, 1), 0)
    wanted = jnp.zeros((slots, 1), jnp.int32)
    base = jnp.zeros((slots, 1), jnp.int32)
    for e in range(slots // CAP):
        inside = row >= e * CAP
        wanted = jnp.where(inside, placement[e], wanted)
        base = jnp.where(inside, e * CAP, base)
    return wanted, row - base


def fetch(pairs, sems):
    copies = [pltpu.make_async_copy(x, y, sems.at[i]) for i, (x, y) in enumerate(pairs)]
    for copy in copies:
        copy.start()
    return copies


def head_kernel(*refs):
    given, (rows, select, weighted), kept = refs[:5], refs[5:8], refs[8:13]
    copies = fetch(zip(given, kept), refs[13])
    placement, routes, gates, tokens, cot = kept
    for copy in copies[:3]:
        copy.wait()
    slots, tok_count = select.shape
    top_count = routes.shape[0]
    half = tokens.shape[1]
    wanted, slot = wanted_column(placement, slots)
    hit = jnp.zeros((slots, tok_count), F32)
    weight = jnp.zeros((slots, tok_count), F32)
    for k in range(top_count):
        match = routes[k : k + 1, :] == wanted
        hit = jnp.where(match, 1.0, hit)
        weight = jnp.where(match, gates[k : k + 1, :].astype(F32), weight)
    row_id = lax.broadcasted_iota(jnp.int32, (tok_count, tok_count), 0)
    col_id = lax.broadcasted_iota(jnp.int32, (tok_count, tok_count), 1)
    before = jnp.where(row_id < col_id, 1.0, 0.0).astype(BF)
    earlier = jnp.dot(hit.astype(BF), before, preferred_element_type=F32)
    live = (hit > 0.0) & (earlier == slot.astype(F32))
    chosen = jnp.where(live, 1.0, 0.0).astype(BF)
    scaled = jnp.where(live, weight, 0.0).astype(BF)
    select[...] = chosen
    weighted[...] = scaled
    copies[3].wait()
    rows[:, :half] = jnp.dot(chosen, tokens[...], preferred_element_type=F32).astype(BF)
    copies[4].wait()
    rows[:, half:] = jnp.dot(scaled, cot[...], preferred_element_type=F32).astype(BF)


class Rows:
    def __init__(self, n_d, n_t, own, others, kept):
        self.n_d, self.n_t, self.kept = n_d, n_t, kept
        self.group = n_d // n_t
        self.d, self.t = lax.axis_index("dp"), lax.axis_index("tensor")
        self.half = kept.shape[2]
        self.chunk = self.half // self.group
        kept[self.t] = own
        for s in range(1, n_t):
            kept[lax.rem(self.t - s + n_t, n_t)] = others[s - 1][...]

    def place(self, s):
        where = lax.rem(self.d - s + self.n_d, self.n_d)
        if self.group == 1:
            return where, slice(None)
        col = pl.multiple_of(lax.rem(where, self.group) * self.chunk, LANES)
        return where // self.group, pl.ds(col, self.chunk)

    def times(self, weight):
        value = None
        for s in range(self.n_d):
            side, cols = self.place(s)
            part = jnp.dot(self.kept[side, :, cols], weight(s), preferred_element_type=F32)
            value = part if value is None else value + part
        return value

    def store(self, s, term, results):
        side, cols = self.place(s)
        step = lax.rem(side - self.t + self.n_t, self.n_t)
        for k in range(self.n_t):

            @pl.when(step == k)
            def _():
                results[k][:, cols] = term.astype(BF)


class Weights:
    def __init__(self, n_d, shards, room, sems, order):
        self.n_d, self.room, self.waited = n_d, room, set()
        keys = [(which, s) for which in order for s in range(n_d)]
        pairs = [(shards[which * n_d + s], room.at[which, s]) for which, s in keys]
        self.copies = dict(zip(keys, fetch(pairs, sems)))

    def of(self, which):
        def shard(s):
            if (which, s) not in self.waited:
                self.copies[which, s].wait()
                self.waited.add((which, s))
            return self.room[which, s]

        return shard


def forward_kernel(n_d, n_t, *refs):
    shards, own, others = refs[: 3 * n_d], refs[3 * n_d], refs[3 * n_d + 1 : 3 * n_d + n_t]
    refs = refs[3 * n_d + n_t :]
    (gate_out, up_out, hidden_out), terms, (kept, room, sems) = refs[:3], refs[3:-3], refs[-3:]
    weights = Weights(n_d, shards, room, sems, (0, 1, 2))
    rows = Rows(n_d, n_t, own[:, : kept.shape[2]], others, kept)
    gate, up = rows.times(weights.of(0)), rows.times(weights.of(1))
    hidden = (gate * jax.nn.sigmoid(gate) * up).astype(BF)
    gate_out[...], up_out[...], hidden_out[...] = gate, up, hidden
    down = weights.of(2)
    for s in range(n_d):
        rows.store(s, dot(hidden, down(s), inner), terms)


def backward_kernel(n_d, n_t, *refs):
    shards, own, others = refs[: 3 * n_d], refs[3 * n_d], refs[3 * n_d + 1 : 3 * n_d + n_t]
    refs = refs[3 * n_d + n_t :]
    (gate_in, up_in, hidden_in, units_out), terms = refs[:4], refs[4:-3]
    kept, room, sems = refs[-3:]
    weights = Weights(n_d, shards, room, sems, (2, 0, 1))
    rows = Rows(n_d, n_t, own[:, kept.shape[2] :], others, kept)
    d_hidden = rows.times(weights.of(2))
    gate, up = gate_in[...], up_in[...]
    sig = jax.nn.sigmoid(gate)
    d_gate = (d_hidden * up * sig * (1.0 + gate * (1.0 - sig))).astype(BF)
    d_up = (d_hidden * gate * sig).astype(BF)
    units = gate.shape[1]
    units_out[:, :units] = d_gate
    units_out[:, units : 2 * units] = d_up
    units_out[:, 2 * units :] = hidden_in[...]
    by_gate = [dot(d_gate, weights.of(0)(s), inner) for s in range(n_d)]
    for s in range(n_d):
        rows.store(s, by_gate[s] + dot(d_up, weights.of(1)(s), inner), terms)


def home_kernel(*refs):
    home = refs[-1]
    count = (len(refs) - 1) // 2
    half = home.shape[1] // 2
    for side in range(2):
        value = None
        for ref in refs[side * count : (side + 1) * count]:
            part = ref[...].astype(F32)
            value = part if value is None else value + part
        home[:, side * half : (side + 1) * half] = value.astype(BF)


def gate_kernel(placement, routes, select, cot, back, gate_part):
    slots = select.shape[0]
    half = cot.shape[1]
    wanted, _ = wanted_column(placement, slots)
    scores = dot(back[:, :half], cot[...], inner)
    scores = jnp.where(select[...].astype(F32) > 0.0, scores, 0.0)
    for k in range(routes.shape[0]):
        match = routes[k : k + 1, :] == wanted
        gate_part[k : k + 1, :] = jnp.sum(
            jnp.where(match, scores, 0.0), axis=0, keepdims=True
        )


def combine_kernel(select, weighted, back, layer_out, input_grad):
    half = layer_out.shape[1]
    layer_out[...] = dot(weighted[...], back[:, :half], contract).astype(BF)
    input_grad[...] = dot(select[...], back[:, half:], contract).astype(BF)


def grads_kernel(x, d, units_ref, g_gate, g_up, g_down):
    units = g_gate.shape[1]
    both = dot(x[...], units_ref[:, : 2 * units], contract).astype(BF)
    g_gate[...] = both[:, :units]
    g_up[...] = both[:, units:]
    g_down[...] = dot(d[...], units_ref[:, 2 * units :], contract).astype(BF)


def weight_grads(held, units_held, chunk, units):
    rows = held.shape[0]
    block = next(b for b in (896, 512, 256, LANES) if chunk % b == 0)
    steps = chunk // block
    out = shape((chunk, units), BF)
    spec = pl.BlockSpec((block, units), lambda i: (i, 0))
    return pl.pallas_call(
        grads_kernel,
        grid=(steps,),
        out_shape=[out] * 3,
        in_specs=[
            pl.BlockSpec((rows, block), lambda i: (0, i)),
            pl.BlockSpec((rows, block), lambda i: (0, i + steps)),
            pl.BlockSpec((rows, 3 * units), lambda i: (0, 0)),
        ],
        out_specs=[spec] * 3,
        compiler_params=pltpu.CompilerParams(
            vmem_limit_bytes=(6 << 20) + 3 * rows * 2 * (3 * units + 2 * block)
        ),
        cost_estimate=pl.CostEstimate(
            flops=6 * rows * chunk * units, bytes_accessed=6 * chunk * units, transcendentals=0
        ),
        name="weight_grads",
    )(held, held, units_held)


def on_device(tokens, routes, gates, cotangent, placement, swap_flag, w_gate, w_up, w_down):
    experts = lax.axis_size("expert")
    myself = lax.axis_index("expert")
    lay = Layout()
    places = jnp.arange(experts, dtype=jnp.int32)
    my_flag = jnp.sum(jnp.where(places == myself, swap_flag, 0)) == 1
    wg, wu, wd = w_gate[0], w_up[0], w_down[0]
    chunk, units = wg.shape
    tok_count, top_count = routes.shape
    slots_all = experts * CAP
    half_width = tokens.shape[1]
    routes_t, gates_t = routes.T, gates.T

    outs = [
        shape((slots_all, 2 * half_width), BF),
        shape((slots_all, tok_count), BF),
        shape((slots_all, tok_count), BF),
    ]
    given = (placement, routes_t, gates_t, tokens, cotangent)
    outgoing, select, weighted = call(
        head_kernel,
        outs,
        given,
        None,
        far=len(given),
        scratch=[
            pltpu.SMEM(placement.shape, jnp.int32),
            *(pltpu.VMEM(x.shape, x.dtype) for x in given[1:]),
            pltpu.SemaphoreType.DMA((len(given),)),
        ],
    )
    arrived = exchanged(outgoing, experts)

    own_weights = (wg, wu, wd)
    shards = []
    for own in own_weights:
        shards += [own, *lay.others(own)]
    x_other = lay.flipped([arrived[:, :half_width]] * (lay.n_t - 1))
    d_other = lay.flipped([arrived[:, half_width:]] * (lay.n_t - 1))
    term = shape((slots_all, half_width), BF)
    kept = [
        pltpu.VMEM((lay.n_t, slots_all, half_width), BF),
        pltpu.VMEM((3, lay.n_d, chunk, units), BF),
        pltpu.SemaphoreType.DMA((3 * lay.n_d,)),
    ]
    outs = [shape((slots_all, units), F32)] * 2 + [shape((slots_all, units), BF)]
    room = None
    work = 6 * slots_all * lay.n_d * chunk * units
    gate, up, hidden, *out_terms = call(
        lambda *refs: forward_kernel(lay.n_d, lay.n_t, *refs),
        outs + [term] * lay.n_t,
        (*shards, arrived, *x_other),
        room,
        scratch=kept,
        far=len(shards),
        flops=work,
    )
    units_own, *in_terms = call(
        lambda *refs: backward_kernel(lay.n_d, lay.n_t, *refs),
        [shape((slots_all, 3 * units), BF)] + [term] * lay.n_t,
        (*shards, arrived, *d_other, gate, up, hidden),
        room,
        scratch=kept,
        far=len(shards),
        flops=work,
    )
    out_got = [out_terms[0], *lay.flipped(out_terms[1:])]
    in_got = [in_terms[0], *lay.flipped(in_terms[1:])]
    (home,) = call(
        home_kernel,
        [shape((slots_all, 2 * half_width), BF)],
        (*out_got, *in_got),
        room_for(*out_got, *in_got),
    )
    back = exchanged(home, experts)

    gate_shape = shape((top_count, tok_count), F32)
    (gate_part,) = call(
        gate_kernel,
        [gate_shape],
        (placement, routes_t, select, cotangent, back),
        room_for(cotangent, back),
        smem=1,
    )
    gate_grad = gate_part
    for step in range(1, lay.n_t):
        other = lax.ppermute(
            gate_part, "tensor", [(i, (i + step) % lay.n_t) for i in range(lay.n_t)]
        )
        gate_grad = gate_grad + other
    gate_grad = gate_grad.T
    outs = [shape(tokens.shape, BF)] * 2
    layer_out, input_grad = call(
        combine_kernel, outs, (select, weighted, back), room_for(back, *outs)
    )

    partner = [(i, (i + experts // 2) % experts) for i in range(experts)]
    moved = lax.ppermute(arrived, "expert", partner)
    held = jnp.where(my_flag, moved, arrived)
    if lay.group == 1:
        pieces = held[None]
    else:
        pieces = jnp.moveaxis(held.reshape(slots_all, 2, lay.group, chunk), 2, 0)
        pieces = pieces.reshape(lay.group, slots_all, 2 * chunk)
    held = jnp.concatenate(lay.spread(pieces), axis=0)
    units_moved = lax.ppermute(units_own, "expert", partner)
    units_held = jnp.where(my_flag, units_moved, units_own)
    units_held = lay.gathered(units_held)
    grads = weight_grads(held, units_held, chunk, units)
    return (layer_out, input_grad, gate_grad, grads[0][None], grads[1][None], grads[2][None])


def solution(mesh):
    placed = (
        P(("expert", "dp"), "tensor"),
        P(("expert", "dp"), None),
        P(("expert", "dp"), None),
        P(("expert", "dp"), "tensor"),
        P(),
        P(),
        P("expert", "dp", "tensor"),
        P("expert", "dp", "tensor"),
        P("expert", "dp", "tensor"),
    )


    return jax.shard_map(
        on_device,
        mesh=mesh,
        in_specs=placed,
        out_specs=(
            P(("expert", "dp"), "tensor"),
            P(("expert", "dp"), "tensor"),
            P(("expert", "dp"), None),
            P("expert", "dp", "tensor"),
            P("expert", "dp", "tensor"),
            P("expert", "dp", "tensor"),
        ),
        check_vma=False,
    )
```

```python
import jax
import jax.numpy as jnp
from jax import lax
from jax.experimental import pallas as pl
from jax.experimental.pallas import tpu as pltpu
from jax.sharding import PartitionSpec as P

CAP = 9
MAIN = 8
BF = jnp.bfloat16
F32 = jnp.float32
LANES = 128

contract = (((0,), (0,)), ((), ()))
inner = (((1,), (1,)), ((), ()))


def dot(a, b, dims):
    return lax.dot_general(a, b, dims, preferred_element_type=F32)


def pick(stack, index, count):
    return stack[0] if count == 1 else lax.dynamic_index_in_dim(stack, index, 0, keepdims=False)


class Layout:
    def __init__(self):
        self.n_d = lax.axis_size("dp")
        self.n_t = lax.axis_size("tensor")
        self.group = self.n_d // self.n_t
        self.d = lax.axis_index("dp")
        self.t = lax.axis_index("tensor")
        self.order = (self.d % self.group) * self.n_t + self.t

    def pairs(self, step):
        route = []
        for d in range(self.n_d):
            for t in range(self.n_t):
                half = d // self.group
                data = ((d % self.group) * self.n_t + t + step) % self.n_d
                route.append((data * self.n_t + half, d * self.n_t + t))
        return route

    def canonical(self, blocks):
        if self.group == 1:
            return blocks
        whole = jnp.stack(blocks)
        whole = jnp.take(whole, (jnp.arange(self.n_d) - self.order) % self.n_d, axis=0)
        return [whole[i] for i in range(self.n_d)]

    def spread(self, rows):
        blocks = []
        for step in range(self.n_d):
            target = (self.d - step) % self.n_d
            chunk = pick(rows, target // self.n_t, self.group)
            blocks.append(lax.ppermute(chunk, ("dp", "tensor"), self.pairs(step)))
        return self.canonical(blocks)

    def flipped(self, values):
        got = []
        for step in range(1, self.n_t):
            route = [(i, (i + step) % self.n_t) for i in range(self.n_t)]
            got.append(lax.ppermute(values[step - 1], "tensor", route))
        return got

    def others(self, value):
        got = []
        for step in range(1, self.n_d):
            route = [(i, (i + step) % self.n_d) for i in range(self.n_d)]
            got.append(lax.ppermute(value, "dp", route))
        return got

    def gathered(self, value):
        if self.n_d == 2 and self.group == 1:
            other = lax.ppermute(value, "dp", [(0, 1), (1, 0)])
            first = self.d == self.order
            return jnp.concatenate([jnp.where(first, value, other), jnp.where(first, other, value)])
        return lax.all_gather(value, "dp", axis=0, tiled=True)


def fold_width(cols):
    return -(-cols // (MAIN * LANES)) * LANES


def folded_shape(experts, cols):
    return shape((experts * MAIN, cols + fold_width(cols)), BF)


def fold(main, last, out):
    rows, cols = main.shape
    width = fold_width(cols)
    out[:, :cols] = main.astype(BF)
    row = lax.broadcasted_iota(jnp.int32, (rows, last.shape[0]), 0)
    col = lax.broadcasted_iota(jnp.int32, (rows, last.shape[0]), 1)
    repeat = jnp.where(row // MAIN == col, 1.0, 0.0).astype(BF)
    wide = jnp.dot(repeat, last.astype(BF), preferred_element_type=F32)
    place = lax.broadcasted_iota(jnp.int32, (rows, width), 0) % MAIN
    value = jnp.zeros((rows, width), F32)
    for q in range(cols // width):
        value = jnp.where(place == q, wide[:, q * width : (q + 1) * width], value)
    out[:, cols:] = value.astype(BF)


def unfold(tail, cols):
    rows, width = tail.shape
    experts = rows // MAIN
    row = lax.broadcasted_iota(jnp.int32, (experts, rows), 0)
    col = lax.broadcasted_iota(jnp.int32, (experts, rows), 1)
    pieces = []
    for q in range(cols // width):
        take = jnp.where(col == row * MAIN + q, 1.0, 0.0).astype(BF)
        pieces.append(jnp.dot(take, tail, preferred_element_type=F32))
    return jnp.concatenate(pieces, axis=1)


def exchanged(rows):
    return lax.all_to_all(rows, "expert", split_axis=0, concat_axis=0, tiled=True)


def call(kernel, outs, args, room, smem=0, far=0, scratch=(), flops=0):
    moved = sum(a.size * a.dtype.itemsize for a in args) + sum(
        o.size * o.dtype.itemsize for o in outs
    )
    return pl.pallas_call(
        kernel,
        out_shape=outs,
        in_specs=[pl.BlockSpec(memory_space=pltpu.SMEM)] * smem
        + [pl.BlockSpec(memory_space=pl.ANY)] * far
        + [pl.BlockSpec(memory_space=pltpu.VMEM)] * (len(args) - smem - far),
        out_specs=[pl.BlockSpec(memory_space=pltpu.VMEM)] * len(outs),
        scratch_shapes=scratch,
        compiler_params=pltpu.CompilerParams(vmem_limit_bytes=room),
        cost_estimate=pl.CostEstimate(flops=flops, bytes_accessed=moved, transcendentals=0),
    )(*args)


def room_for(*arrays):
    return (6 << 20) + 3 * sum(a.size * a.dtype.itemsize for a in arrays) // 2


def shape(dims, dtype):
    return jax.ShapeDtypeStruct(dims, dtype)


def wanted_column(placement, slots):
    row = lax.broadcasted_iota(jnp.int32, (slots, 1), 0)
    experts = slots // CAP
    main = row < experts * MAIN
    position = jnp.where(main, row // MAIN, row - experts * MAIN)
    wanted = jnp.zeros((slots, 1), jnp.int32)
    for e in range(experts):
        wanted = jnp.where(position == e, placement[e], wanted)
    return wanted, jnp.where(main, row % MAIN, MAIN)


def fetch(pairs, sems):
    copies = [pltpu.make_async_copy(x, y, sems.at[i]) for i, (x, y) in enumerate(pairs)]
    for copy in copies:
        copy.start()
    return copies


def head_kernel(*refs):
    given, (rows, select, weighted), kept = refs[:5], refs[5:8], refs[8:13]
    copies = fetch(zip(given, kept), refs[13])
    placement, routes, gates, tokens, cot = kept
    for copy in copies[:3]:
        copy.wait()
    slots, tok_count = select.shape
    top_count = routes.shape[0]
    wanted, slot = wanted_column(placement, slots)
    hit = jnp.zeros((slots, tok_count), F32)
    weight = jnp.zeros((slots, tok_count), F32)
    for k in range(top_count):
        match = routes[k : k + 1, :] == wanted
        hit = jnp.where(match, 1.0, hit)
        weight = jnp.where(match, gates[k : k + 1, :].astype(F32), weight)
    row_id = lax.broadcasted_iota(jnp.int32, (tok_count, tok_count), 0)
    col_id = lax.broadcasted_iota(jnp.int32, (tok_count, tok_count), 1)
    before = jnp.where(row_id < col_id, 1.0, 0.0).astype(BF)
    earlier = jnp.dot(hit.astype(BF), before, preferred_element_type=F32)
    live = (hit > 0.0) & (earlier == slot.astype(F32))
    chosen = jnp.where(live, 1.0, 0.0).astype(BF)
    scaled = jnp.where(live, weight, 0.0).astype(BF)
    select[...] = chosen
    weighted[...] = scaled
    copies[3].wait()
    x = jnp.dot(chosen, tokens[...], preferred_element_type=F32)
    copies[4].wait()
    d = jnp.dot(scaled, cot[...], preferred_element_type=F32)
    both = jnp.concatenate([x, d], axis=1)
    main = rows.shape[0]
    fold(both[:main], both[main:], rows)


def split_kernel(rows, x, d):
    main, half = rows.shape[0], x.shape[1]
    last = unfold(rows[:, 2 * half :], 2 * half).astype(BF)
    for side, out in ((0, x), (1, d)):
        out[:main] = rows[:, side * half : (side + 1) * half]
        out[main:] = last[:, side * half : (side + 1) * half]


def held_kernel(flag, moved, own, out):
    main, cols = own.shape[0], out.shape[1]
    mine = flag[lax.axis_index("expert")] != 1

    def put(ref):
        out[:main] = ref[:, :cols]
        out[main:] = unfold(ref[:, cols:], cols).astype(BF)

    @pl.when(mine)
    def _():
        put(own)

    @pl.when(jnp.logical_not(mine))
    def _():
        put(moved)


class Rows:
    def __init__(self, n_d, n_t, own, others, kept):
        self.n_d, self.n_t, self.kept = n_d, n_t, kept
        self.group = n_d // n_t
        self.d, self.t = lax.axis_index("dp"), lax.axis_index("tensor")
        self.half = kept.shape[2]
        self.chunk = self.half // self.group
        kept[self.t] = own
        for s in range(1, n_t):
            kept[lax.rem(self.t - s + n_t, n_t)] = others[s - 1][...]

    def place(self, s):
        where = lax.rem(self.d - s + self.n_d, self.n_d)
        if self.group == 1:
            return where, slice(None)
        col = pl.multiple_of(lax.rem(where, self.group) * self.chunk, LANES)
        return where // self.group, pl.ds(col, self.chunk)

    def times(self, weight):
        value = None
        for s in range(self.n_d):
            side, cols = self.place(s)
            part = jnp.dot(self.kept[side, :, cols], weight(s), preferred_element_type=F32)
            value = part if value is None else value + part
        return value

    def store(self, s, term, results):
        side, cols = self.place(s)
        step = lax.rem(side - self.t + self.n_t, self.n_t)
        for k in range(self.n_t):

            @pl.when(step == k)
            def _():
                results[k][:, cols] = term.astype(BF)


class Weights:
    def __init__(self, n_d, shards, room, sems, order):
        self.n_d, self.room, self.waited = n_d, room, set()
        keys = [(which, s) for which in order for s in range(n_d)]
        pairs = [(shards[which * n_d + s], room.at[which, s]) for which, s in keys]
        self.copies = dict(zip(keys, fetch(pairs, sems)))

    def of(self, which):
        def shard(s):
            if (which, s) not in self.waited:
                self.copies[which, s].wait()
                self.waited.add((which, s))
            return self.room[which, s]

        return shard


def forward_kernel(n_d, n_t, *refs):
    shards, own, others = refs[: 3 * n_d], refs[3 * n_d], refs[3 * n_d + 1 : 3 * n_d + n_t]
    refs = refs[3 * n_d + n_t :]
    (gate_out, up_out, hidden_out), terms, (kept, room, sems) = refs[:3], refs[3:-3], refs[-3:]
    weights = Weights(n_d, shards, room, sems, (0, 1, 2))
    rows = Rows(n_d, n_t, own[...], others, kept)
    gate, up = rows.times(weights.of(0)), rows.times(weights.of(1))
    hidden = (gate * jax.nn.sigmoid(gate) * up).astype(BF)
    gate_out[...], up_out[...], hidden_out[...] = gate, up, hidden
    down = weights.of(2)
    for s in range(n_d):
        rows.store(s, dot(hidden, down(s), inner), terms)


def backward_kernel(n_d, n_t, *refs):
    shards, own, others = refs[: 3 * n_d], refs[3 * n_d], refs[3 * n_d + 1 : 3 * n_d + n_t]
    refs = refs[3 * n_d + n_t :]
    (gate_in, up_in, hidden_in, units_out), terms = refs[:4], refs[4:-3]
    kept, room, sems = refs[-3:]
    weights = Weights(n_d, shards, room, sems, (2, 0, 1))
    rows = Rows(n_d, n_t, own[...], others, kept)
    d_hidden = rows.times(weights.of(2))
    gate, up = gate_in[...], up_in[...]
    sig = jax.nn.sigmoid(gate)
    d_gate = (d_hidden * up * sig * (1.0 + gate * (1.0 - sig))).astype(BF)
    d_up = (d_hidden * gate * sig).astype(BF)
    units = gate.shape[1]
    units_out[:, :units] = d_gate
    units_out[:, units : 2 * units] = d_up
    units_out[:, 2 * units :] = hidden_in[...]
    by_gate = [dot(d_gate, weights.of(0)(s), inner) for s in range(n_d)]
    for s in range(n_d):
        rows.store(s, by_gate[s] + dot(d_up, weights.of(1)(s), inner), terms)


def home_kernel(*refs):
    home = refs[-1]
    count = (len(refs) - 1) // 2
    sides = []
    for side in range(2):
        value = None
        for ref in refs[side * count : (side + 1) * count]:
            part = ref[...].astype(F32)
            value = part if value is None else value + part
        sides.append(value)
    both = jnp.concatenate(sides, axis=1)
    main = home.shape[0]
    fold(both[:main], both[main:], home)


def gate_kernel(placement, routes, select, cot, back, gate_part):
    slots = select.shape[0]
    half = cot.shape[1]
    wanted, _ = wanted_column(placement, slots)
    last = unfold(back[:, 2 * half :], 2 * half)[:, :half].astype(BF)
    scores = jnp.concatenate([dot(back[:, :half], cot[...], inner), dot(last, cot[...], inner)])
    scores = jnp.where(select[...].astype(F32) > 0.0, scores, 0.0)
    for k in range(routes.shape[0]):
        match = routes[k : k + 1, :] == wanted
        gate_part[k : k + 1, :] = jnp.sum(
            jnp.where(match, scores, 0.0), axis=0, keepdims=True
        )


def combine_kernel(select, weighted, back, layer_out, input_grad):
    main, half = back.shape[0], layer_out.shape[1]
    last = unfold(back[:, 2 * half :], 2 * half).astype(BF)
    for side, weight, out in ((0, weighted, layer_out), (1, select, input_grad)):
        cols = slice(side * half, (side + 1) * half)
        value = dot(weight[:main], back[:, cols], contract)
        out[...] = (value + dot(weight[main:], last[:, cols], contract)).astype(BF)


def grads_kernel(count, *refs):
    held, kept_units, (g_gate, g_up, g_down) = refs[: 2 * count], refs[2 * count], refs[-3:]
    units = g_gate.shape[1]

    def joined(blocks):
        return jnp.concatenate([x[...].astype(F32) for x in blocks]).astype(BF)

    both = dot(joined(held[:count]), kept_units[:, : 2 * units], contract).astype(BF)
    g_gate[...] = both[:, :units]
    g_up[...] = both[:, units:]
    g_down[...] = dot(joined(held[count:]), kept_units[:, 2 * units :], contract).astype(BF)


def weight_grads(held, units_held, chunk, units):
    count, rows = len(held), held[0].shape[0]
    block = next(b for b in (896, 512, 256, LANES) if chunk % b == 0)
    steps = chunk // block
    out = shape((chunk, units), BF)
    spec = pl.BlockSpec((block, units), lambda i: (i, 0))
    x_spec = pl.BlockSpec((rows, block), lambda i: (0, i))
    d_spec = pl.BlockSpec((rows, block), lambda i: (0, i + steps))
    return pl.pallas_call(
        lambda *refs: grads_kernel(count, *refs),
        grid=(steps,),
        out_shape=[out] * 3,
        in_specs=[x_spec] * count
        + [d_spec] * count
        + [pl.BlockSpec((count * rows, 3 * units), lambda i: (0, 0))],
        out_specs=[spec] * 3,
        compiler_params=pltpu.CompilerParams(
            vmem_limit_bytes=(12 << 20) + 6 * count * rows * 2 * (3 * units + 2 * block)
        ),
        cost_estimate=pl.CostEstimate(
            flops=6 * count * rows * chunk * units,
            bytes_accessed=6 * chunk * units,
            transcendentals=0,
        ),
        name="weight_grads",
    )(*held, *held, units_held)


def on_device(tokens, routes, gates, cotangent, placement, swap_flag, w_gate, w_up, w_down):
    experts = lax.axis_size("expert")
    myself = lax.axis_index("expert")
    lay = Layout()
    places = jnp.arange(experts, dtype=jnp.int32)
    my_flag = jnp.sum(jnp.where(places == myself, swap_flag, 0)) == 1
    wg, wu, wd = w_gate[0], w_up[0], w_down[0]
    chunk, units = wg.shape
    tok_count, top_count = routes.shape
    slots_all = experts * CAP
    half_width = tokens.shape[1]
    routes_t, gates_t = routes.T, gates.T

    outs = [
        folded_shape(experts, 2 * half_width),
        shape((slots_all, tok_count), BF),
        shape((slots_all, tok_count), BF),
    ]
    given = (placement, routes_t, gates_t, tokens, cotangent)
    outgoing, select, weighted = call(
        head_kernel,
        outs,
        given,
        None,
        far=len(given),
        scratch=[
            pltpu.SMEM(placement.shape, jnp.int32),
            *(pltpu.VMEM(x.shape, x.dtype) for x in given[1:]),
            pltpu.SemaphoreType.DMA((len(given),)),
        ],
    )
    arrived = exchanged(outgoing)
    sides = [shape((slots_all, half_width), BF)] * 2
    x_own, d_own = call(split_kernel, sides, (arrived,), room_for(*sides, *sides))

    own_weights = (wg, wu, wd)
    shards = []
    for own in own_weights:
        shards += [own, *lay.others(own)]
    x_other = lay.flipped([x_own] * (lay.n_t - 1))
    d_other = lay.flipped([d_own] * (lay.n_t - 1))
    term = shape((slots_all, half_width), BF)
    kept = [
        pltpu.VMEM((lay.n_t, slots_all, half_width), BF),
        pltpu.VMEM((3, lay.n_d, chunk, units), BF),
        pltpu.SemaphoreType.DMA((3 * lay.n_d,)),
    ]
    outs = [shape((slots_all, units), F32)] * 2 + [shape((slots_all, units), BF)]
    room = 52 << 20
    work = 6 * slots_all * lay.n_d * chunk * units
    gate, up, hidden, *out_terms = call(
        lambda *refs: forward_kernel(lay.n_d, lay.n_t, *refs),
        outs + [term] * lay.n_t,
        (*shards, x_own, *x_other),
        room,
        scratch=kept,
        far=len(shards),
        flops=work,
    )
    units_own, *in_terms = call(
        lambda *refs: backward_kernel(lay.n_d, lay.n_t, *refs),
        [shape((slots_all, 3 * units), BF)] + [term] * lay.n_t,
        (*shards, d_own, *d_other, gate, up, hidden),
        room,
        scratch=kept,
        far=len(shards),
        flops=work,
    )
    out_got = [out_terms[0], *lay.flipped(out_terms[1:])]
    in_got = [in_terms[0], *lay.flipped(in_terms[1:])]
    (home,) = call(
        home_kernel,
        [folded_shape(experts, 2 * half_width)],
        (*out_got, *in_got),
        room_for(*out_got, *in_got, *out_got, *in_got),
    )
    back = exchanged(home)

    gate_shape = shape((top_count, tok_count), F32)
    (gate_part,) = call(
        gate_kernel,
        [gate_shape],
        (placement, routes_t, select, cotangent, back),
        room_for(cotangent, back),
        smem=1,
    )
    gate_grad = gate_part
    for step in range(1, lay.n_t):
        other = lax.ppermute(
            gate_part, "tensor", [(i, (i + step) % lay.n_t) for i in range(lay.n_t)]
        )
        gate_grad = gate_grad + other
    gate_grad = gate_grad.T
    outs = [shape(tokens.shape, BF)] * 2
    layer_out, input_grad = call(
        combine_kernel, outs, (select, weighted, back), room_for(back, *outs)
    )

    partner = [(i, (i + experts // 2) % experts) for i in range(experts)]
    moved = lax.ppermute(arrived, "expert", partner)
    both = shape((slots_all, 2 * half_width), BF)
    (held,) = call(
        held_kernel, [both], (swap_flag, moved, arrived), room_for(both, both, both), smem=1
    )
    if lay.group == 1:
        pieces = held[None]
    else:
        pieces = jnp.moveaxis(held.reshape(slots_all, 2, lay.group, chunk), 2, 0)
        pieces = pieces.reshape(lay.group, slots_all, 2 * chunk)
    held = lay.spread(pieces)
    units_moved = lax.ppermute(units_own, "expert", partner)
    units_held = jnp.where(my_flag, units_moved, units_own)
    units_held = lay.gathered(units_held)
    grads = weight_grads(held, units_held, chunk, units)
    return (layer_out, input_grad, gate_grad, grads[0][None], grads[1][None], grads[2][None])


def solution(mesh):
    placed = (
        P(("expert", "dp"), "tensor"),
        P(("expert", "dp"), None),
        P(("expert", "dp"), None),
        P(("expert", "dp"), "tensor"),
        P(),
        P(),
        P("expert", "dp", "tensor"),
        P("expert", "dp", "tensor"),
        P("expert", "dp", "tensor"),
    )


    return jax.shard_map(
        on_device,
        mesh=mesh,
        in_specs=placed,
        out_specs=(
            P(("expert", "dp"), "tensor"),
            P(("expert", "dp"), "tensor"),
            P(("expert", "dp"), None),
            P("expert", "dp", "tensor"),
            P("expert", "dp", "tensor"),
            P("expert", "dp", "tensor"),
        ),
        check_vma=False,
    )
```

```python
import jax
import jax.numpy as jnp
from jax import lax
from jax.experimental import pallas as pl
from jax.experimental.pallas import tpu as pltpu
from jax.sharding import PartitionSpec as P

CAP = 9
MAIN = 8
BF = jnp.bfloat16
F32 = jnp.float32
LANES = 128

contract = (((0,), (0,)), ((), ()))
inner = (((1,), (1,)), ((), ()))


def dot(a, b, dims):
    return lax.dot_general(a, b, dims, preferred_element_type=F32)


def pick(stack, index, count):
    return stack[0] if count == 1 else lax.dynamic_index_in_dim(stack, index, 0, keepdims=False)


class Layout:
    def __init__(self):
        self.n_d = lax.axis_size("dp")
        self.n_t = lax.axis_size("tensor")
        self.group = self.n_d // self.n_t
        self.d = lax.axis_index("dp")
        self.t = lax.axis_index("tensor")
        self.order = (self.d % self.group) * self.n_t + self.t

    def pairs(self, step):
        route = []
        for d in range(self.n_d):
            for t in range(self.n_t):
                half = d // self.group
                data = ((d % self.group) * self.n_t + t + step) % self.n_d
                route.append((data * self.n_t + half, d * self.n_t + t))
        return route

    def canonical(self, blocks):
        if self.group == 1:
            return blocks
        whole = jnp.stack(blocks)
        whole = jnp.take(whole, (jnp.arange(self.n_d) - self.order) % self.n_d, axis=0)
        return [whole[i] for i in range(self.n_d)]

    def spread(self, rows):
        blocks = []
        for step in range(self.n_d):
            target = (self.d - step) % self.n_d
            chunk = pick(rows, target // self.n_t, self.group)
            blocks.append(lax.ppermute(chunk, ("dp", "tensor"), self.pairs(step)))
        return self.canonical(blocks)

    def flipped(self, values):
        got = []
        for step in range(1, self.n_t):
            route = [(i, (i + step) % self.n_t) for i in range(self.n_t)]
            got.append(lax.ppermute(values[step - 1], "tensor", route))
        return got

    def others(self, value):
        got = []
        for step in range(1, self.n_d):
            route = [(i, (i + step) % self.n_d) for i in range(self.n_d)]
            got.append(lax.ppermute(value, "dp", route))
        return got

    def gathered(self, value):
        if self.n_d == 2 and self.group == 1:
            other = lax.ppermute(value, "dp", [(0, 1), (1, 0)])
            first = self.d == self.order
            return jnp.concatenate([jnp.where(first, value, other), jnp.where(first, other, value)])
        return lax.all_gather(value, "dp", axis=0, tiled=True)


def fold_width(cols):
    return -(-cols // (MAIN * LANES)) * LANES


def folded_shape(experts, cols):
    return shape((experts * MAIN, cols + fold_width(cols)), BF)


def fold(main, last, out):
    rows, cols = main.shape
    width = fold_width(cols)
    out[:, :cols] = main.astype(BF)
    row = lax.broadcasted_iota(jnp.int32, (rows, last.shape[0]), 0)
    col = lax.broadcasted_iota(jnp.int32, (rows, last.shape[0]), 1)
    repeat = jnp.where(row // MAIN == col, 1.0, 0.0).astype(BF)
    wide = jnp.dot(repeat, last.astype(BF), preferred_element_type=F32)
    place = lax.broadcasted_iota(jnp.int32, (rows, width), 0) % MAIN
    value = jnp.zeros((rows, width), F32)
    for q in range(cols // width):
        value = jnp.where(place == q, wide[:, q * width : (q + 1) * width], value)
    out[:, cols:] = value.astype(BF)


def unfold(tail, cols):
    rows, width = tail.shape
    experts = rows // MAIN
    row = lax.broadcasted_iota(jnp.int32, (experts, rows), 0)
    col = lax.broadcasted_iota(jnp.int32, (experts, rows), 1)
    pieces = []
    for q in range(cols // width):
        take = jnp.where(col == row * MAIN + q, 1.0, 0.0).astype(BF)
        pieces.append(jnp.dot(take, tail, preferred_element_type=F32))
    return jnp.concatenate(pieces, axis=1)


def exchanged(rows):
    return lax.all_to_all(rows, "expert", split_axis=0, concat_axis=0, tiled=True)


def call(kernel, outs, args, room, smem=0, far=0, scratch=(), flops=0):
    moved = sum(a.size * a.dtype.itemsize for a in args) + sum(
        o.size * o.dtype.itemsize for o in outs
    )
    return pl.pallas_call(
        kernel,
        out_shape=outs,
        in_specs=[pl.BlockSpec(memory_space=pltpu.SMEM)] * smem
        + [pl.BlockSpec(memory_space=pl.ANY)] * far
        + [pl.BlockSpec(memory_space=pltpu.VMEM)] * (len(args) - smem - far),
        out_specs=[pl.BlockSpec(memory_space=pltpu.VMEM)] * len(outs),
        scratch_shapes=scratch,
        compiler_params=pltpu.CompilerParams(vmem_limit_bytes=room),
        cost_estimate=pl.CostEstimate(flops=flops, bytes_accessed=moved, transcendentals=0),
    )(*args)


def room_for(*arrays):
    return (6 << 20) + 3 * sum(a.size * a.dtype.itemsize for a in arrays) // 2


def shape(dims, dtype):
    return jax.ShapeDtypeStruct(dims, dtype)


def wanted_column(placement, slots):
    row = lax.broadcasted_iota(jnp.int32, (slots, 1), 0)
    experts = slots // CAP
    main = row < experts * MAIN
    position = jnp.where(main, row // MAIN, row - experts * MAIN)
    wanted = jnp.zeros((slots, 1), jnp.int32)
    for e in range(experts):
        wanted = jnp.where(position == e, placement[e], wanted)
    return wanted, jnp.where(main, row % MAIN, MAIN)


def fetch(pairs, sems):
    copies = [pltpu.make_async_copy(x, y, sems.at[i]) for i, (x, y) in enumerate(pairs)]
    for copy in copies:
        copy.start()
    return copies


def head_kernel(*refs):
    given, (rows, select, weighted), kept = refs[:5], refs[5:8], refs[8:13]
    copies = fetch(zip(given, kept), refs[13])
    placement, routes, gates, tokens, cot = kept
    for copy in copies[:3]:
        copy.wait()
    slots, tok_count = select.shape
    top_count = routes.shape[0]
    wanted, slot = wanted_column(placement, slots)
    hit = jnp.zeros((slots, tok_count), F32)
    weight = jnp.zeros((slots, tok_count), F32)
    for k in range(top_count):
        match = routes[k : k + 1, :] == wanted
        hit = jnp.where(match, 1.0, hit)
        weight = jnp.where(match, gates[k : k + 1, :].astype(F32), weight)
    row_id = lax.broadcasted_iota(jnp.int32, (tok_count, tok_count), 0)
    col_id = lax.broadcasted_iota(jnp.int32, (tok_count, tok_count), 1)
    before = jnp.where(row_id < col_id, 1.0, 0.0).astype(BF)
    earlier = jnp.dot(hit.astype(BF), before, preferred_element_type=F32)
    live = (hit > 0.0) & (earlier == slot.astype(F32))
    chosen = jnp.where(live, 1.0, 0.0).astype(BF)
    scaled = jnp.where(live, weight, 0.0).astype(BF)
    select[...] = chosen
    weighted[...] = scaled
    copies[3].wait()
    x = jnp.dot(chosen, tokens[...], preferred_element_type=F32)
    copies[4].wait()
    d = jnp.dot(scaled, cot[...], preferred_element_type=F32)
    both = jnp.concatenate([x, d], axis=1)
    main = rows.shape[0]
    fold(both[:main], both[main:], rows)


def split_kernel(rows, x, d):
    main, half = rows.shape[0], x.shape[1]
    last = unfold(rows[:, 2 * half :], 2 * half).astype(BF)
    for side, out in ((0, x), (1, d)):
        out[:main] = rows[:, side * half : (side + 1) * half]
        out[main:] = last[:, side * half : (side + 1) * half]


def held_kernel(flag, moved, near, own, out, both):
    main, cols = own.shape[0], out.shape[1]
    half = main // 2
    me = lax.axis_index("expert")
    mine = flag[me] != 1
    side = me // (lax.axis_size("expert") // 2)

    @pl.when(mine)
    def _():
        both[...] = own[...]

    @pl.when(jnp.logical_not(mine))
    def _():
        both[pl.ds(pl.multiple_of(side * half, half), half)] = near[...]
        both[pl.ds(pl.multiple_of((1 - side) * half, half), half)] = moved[...]

    out[:main] = both[:, :cols]
    out[main:] = unfold(both[:, cols:], cols).astype(BF)


class Rows:
    def __init__(self, n_d, n_t, own, others, kept):
        self.n_d, self.n_t, self.kept = n_d, n_t, kept
        self.group = n_d // n_t
        self.d, self.t = lax.axis_index("dp"), lax.axis_index("tensor")
        self.half = kept.shape[2]
        self.chunk = self.half // self.group
        kept[self.t] = own
        for s in range(1, n_t):
            kept[lax.rem(self.t - s + n_t, n_t)] = others[s - 1][...]

    def place(self, s):
        where = lax.rem(self.d - s + self.n_d, self.n_d)
        if self.group == 1:
            return where, slice(None)
        col = pl.multiple_of(lax.rem(where, self.group) * self.chunk, LANES)
        return where // self.group, pl.ds(col, self.chunk)

    def times(self, weight):
        value = None
        for s in range(self.n_d):
            side, cols = self.place(s)
            part = jnp.dot(self.kept[side, :, cols], weight(s), preferred_element_type=F32)
            value = part if value is None else value + part
        return value

    def store(self, s, term, results):
        side, cols = self.place(s)
        step = lax.rem(side - self.t + self.n_t, self.n_t)
        for k in range(self.n_t):

            @pl.when(step == k)
            def _():
                results[k][:, cols] = term.astype(BF)


class Weights:
    def __init__(self, n_d, shards, room, sems, order):
        self.n_d, self.room, self.waited = n_d, room, set()
        keys = [(which, s) for which in order for s in range(n_d)]
        pairs = [(shards[which * n_d + s], room.at[which, s]) for which, s in keys]
        self.copies = dict(zip(keys, fetch(pairs, sems)))

    def of(self, which):
        def shard(s):
            if (which, s) not in self.waited:
                self.copies[which, s].wait()
                self.waited.add((which, s))
            return self.room[which, s]

        return shard


def forward_kernel(n_d, n_t, *refs):
    shards, own, others = refs[: 3 * n_d], refs[3 * n_d], refs[3 * n_d + 1 : 3 * n_d + n_t]
    refs = refs[3 * n_d + n_t :]
    (gate_out, up_out, hidden_out), terms, (kept, room, sems) = refs[:3], refs[3:-3], refs[-3:]
    weights = Weights(n_d, shards, room, sems, (0, 1, 2))
    rows = Rows(n_d, n_t, own[...], others, kept)
    gate, up = rows.times(weights.of(0)), rows.times(weights.of(1))
    hidden = (gate * jax.nn.sigmoid(gate) * up).astype(BF)
    gate_out[...], up_out[...], hidden_out[...] = gate, up, hidden
    down = weights.of(2)
    for s in range(n_d):
        rows.store(s, dot(hidden, down(s), inner), terms)


def backward_kernel(n_d, n_t, *refs):
    shards, own, others = refs[: 3 * n_d], refs[3 * n_d], refs[3 * n_d + 1 : 3 * n_d + n_t]
    refs = refs[3 * n_d + n_t :]
    (gate_in, up_in, hidden_in, units_out), terms = refs[:4], refs[4:-3]
    kept, room, sems = refs[-3:]
    weights = Weights(n_d, shards, room, sems, (2, 0, 1))
    rows = Rows(n_d, n_t, own[...], others, kept)
    d_hidden = rows.times(weights.of(2))
    gate, up = gate_in[...], up_in[...]
    sig = jax.nn.sigmoid(gate)
    d_gate = (d_hidden * up * sig * (1.0 + gate * (1.0 - sig))).astype(BF)
    d_up = (d_hidden * gate * sig).astype(BF)
    units = gate.shape[1]
    units_out[:, :units] = d_gate
    units_out[:, units : 2 * units] = d_up
    units_out[:, 2 * units :] = hidden_in[...]
    by_gate = [dot(d_gate, weights.of(0)(s), inner) for s in range(n_d)]
    for s in range(n_d):
        rows.store(s, by_gate[s] + dot(d_up, weights.of(1)(s), inner), terms)


def home_kernel(*refs):
    home = refs[-1]
    count = (len(refs) - 1) // 2
    sides = []
    for side in range(2):
        value = None
        for ref in refs[side * count : (side + 1) * count]:
            part = ref[...].astype(F32)
            value = part if value is None else value + part
        sides.append(value)
    both = jnp.concatenate(sides, axis=1)
    main = home.shape[0]
    fold(both[:main], both[main:], home)


def gate_kernel(placement, routes, select, cot, back, gate_part):
    slots = select.shape[0]
    half = cot.shape[1]
    wanted, _ = wanted_column(placement, slots)
    last = unfold(back[:, 2 * half :], 2 * half)[:, :half].astype(BF)
    scores = jnp.concatenate([dot(back[:, :half], cot[...], inner), dot(last, cot[...], inner)])
    scores = jnp.where(select[...].astype(F32) > 0.0, scores, 0.0)
    for k in range(routes.shape[0]):
        match = routes[k : k + 1, :] == wanted
        gate_part[k : k + 1, :] = jnp.sum(
            jnp.where(match, scores, 0.0), axis=0, keepdims=True
        )


def combine_kernel(select, weighted, back, layer_out, input_grad):
    main, half = back.shape[0], layer_out.shape[1]
    last = unfold(back[:, 2 * half :], 2 * half).astype(BF)
    for side, weight, out in ((0, weighted, layer_out), (1, select, input_grad)):
        cols = slice(side * half, (side + 1) * half)
        value = dot(weight[:main], back[:, cols], contract)
        out[...] = (value + dot(weight[main:], last[:, cols], contract)).astype(BF)


def grads_kernel(count, *refs):
    held, kept_units, (g_gate, g_up, g_down) = refs[: 2 * count], refs[2 * count], refs[-3:]
    units = g_gate.shape[1]

    def joined(blocks):
        return jnp.concatenate([x[...].astype(F32) for x in blocks]).astype(BF)

    both = dot(joined(held[:count]), kept_units[:, : 2 * units], contract).astype(BF)
    g_gate[...] = both[:, :units]
    g_up[...] = both[:, units:]
    g_down[...] = dot(joined(held[count:]), kept_units[:, 2 * units :], contract).astype(BF)


def weight_grads(held, units_held, chunk, units):
    count, rows = len(held), held[0].shape[0]
    block = next(b for b in (896, 512, 256, LANES) if chunk % b == 0)
    steps = chunk // block
    out = shape((chunk, units), BF)
    spec = pl.BlockSpec((block, units), lambda i: (i, 0))
    x_spec = pl.BlockSpec((rows, block), lambda i: (0, i))
    d_spec = pl.BlockSpec((rows, block), lambda i: (0, i + steps))
    return pl.pallas_call(
        lambda *refs: grads_kernel(count, *refs),
        grid=(steps,),
        out_shape=[out] * 3,
        in_specs=[x_spec] * count
        + [d_spec] * count
        + [pl.BlockSpec((count * rows, 3 * units), lambda i: (0, 0))],
        out_specs=[spec] * 3,
        compiler_params=pltpu.CompilerParams(
            vmem_limit_bytes=(12 << 20) + 6 * count * rows * 2 * (3 * units + 2 * block)
        ),
        cost_estimate=pl.CostEstimate(
            flops=6 * count * rows * chunk * units,
            bytes_accessed=6 * chunk * units,
            transcendentals=0,
        ),
        name="weight_grads",
    )(*held, *held, units_held)


def on_device(tokens, routes, gates, cotangent, placement, swap_flag, w_gate, w_up, w_down):
    experts = lax.axis_size("expert")
    myself = lax.axis_index("expert")
    lay = Layout()
    places = jnp.arange(experts, dtype=jnp.int32)
    my_flag = jnp.sum(jnp.where(places == myself, swap_flag, 0)) == 1
    wg, wu, wd = w_gate[0], w_up[0], w_down[0]
    chunk, units = wg.shape
    tok_count, top_count = routes.shape
    slots_all = experts * CAP
    half_width = tokens.shape[1]
    routes_t, gates_t = routes.T, gates.T

    outs = [
        folded_shape(experts, 2 * half_width),
        shape((slots_all, tok_count), BF),
        shape((slots_all, tok_count), BF),
    ]
    given = (placement, routes_t, gates_t, tokens, cotangent)
    outgoing, select, weighted = call(
        head_kernel,
        outs,
        given,
        None,
        far=len(given),
        scratch=[
            pltpu.SMEM(placement.shape, jnp.int32),
            *(pltpu.VMEM(x.shape, x.dtype) for x in given[1:]),
            pltpu.SemaphoreType.DMA((len(given),)),
        ],
    )
    arrived = exchanged(outgoing)
    half_axis = experts // 2
    side = myself // half_axis

    def of_half(rows, which):
        count = half_axis * MAIN
        return lax.dynamic_slice_in_dim(rows, which * count, count, axis=0)

    near = lax.all_to_all(
        of_half(outgoing, 1 - side),
        "expert",
        split_axis=0,
        concat_axis=0,
        axis_index_groups=[list(range(half_axis)), list(range(half_axis, experts))],
        tiled=True,
    )
    sides = [shape((slots_all, half_width), BF)] * 2
    x_own, d_own = call(split_kernel, sides, (arrived,), room_for(*sides, *sides))

    own_weights = (wg, wu, wd)
    shards = []
    for own in own_weights:
        shards += [own, *lay.others(own)]
    x_other = lay.flipped([x_own] * (lay.n_t - 1))
    d_other = lay.flipped([d_own] * (lay.n_t - 1))
    term = shape((slots_all, half_width), BF)
    kept = [
        pltpu.VMEM((lay.n_t, slots_all, half_width), BF),
        pltpu.VMEM((3, lay.n_d, chunk, units), BF),
        pltpu.SemaphoreType.DMA((3 * lay.n_d,)),
    ]
    outs = [shape((slots_all, units), F32)] * 2 + [shape((slots_all, units), BF)]
    room = 52 << 20
    work = 6 * slots_all * lay.n_d * chunk * units
    gate, up, hidden, *out_terms = call(
        lambda *refs: forward_kernel(lay.n_d, lay.n_t, *refs),
        outs + [term] * lay.n_t,
        (*shards, x_own, *x_other),
        room,
        scratch=kept,
        far=len(shards),
        flops=work,
    )
    units_own, *in_terms = call(
        lambda *refs: backward_kernel(lay.n_d, lay.n_t, *refs),
        [shape((slots_all, 3 * units), BF)] + [term] * lay.n_t,
        (*shards, d_own, *d_other, gate, up, hidden),
        room,
        scratch=kept,
        far=len(shards),
        flops=work,
    )
    out_got = [out_terms[0], *lay.flipped(out_terms[1:])]
    in_got = [in_terms[0], *lay.flipped(in_terms[1:])]
    (home,) = call(
        home_kernel,
        [folded_shape(experts, 2 * half_width)],
        (*out_got, *in_got),
        room_for(*out_got, *in_got, *out_got, *in_got),
    )
    back = exchanged(home)

    gate_shape = shape((top_count, tok_count), F32)
    (gate_part,) = call(
        gate_kernel,
        [gate_shape],
        (placement, routes_t, select, cotangent, back),
        room_for(cotangent, back),
        smem=1,
    )
    gate_grad = gate_part
    for step in range(1, lay.n_t):
        other = lax.ppermute(
            gate_part, "tensor", [(i, (i + step) % lay.n_t) for i in range(lay.n_t)]
        )
        gate_grad = gate_grad + other
    gate_grad = gate_grad.T
    outs = [shape(tokens.shape, BF)] * 2
    layer_out, input_grad = call(
        combine_kernel, outs, (select, weighted, back), room_for(back, *outs)
    )

    partner = [(i, (i + experts // 2) % experts) for i in range(experts)]
    moved = lax.ppermute(of_half(arrived, side), "expert", partner)
    both = shape((slots_all, 2 * half_width), BF)
    (held,) = call(
        held_kernel,
        [both],
        (swap_flag, moved, near, arrived),
        room_for(both, both, both, both),
        smem=1,
        scratch=[pltpu.VMEM(arrived.shape, BF)],
    )
    if lay.group == 1:
        pieces = held[None]
    else:
        pieces = jnp.moveaxis(held.reshape(slots_all, 2, lay.group, chunk), 2, 0)
        pieces = pieces.reshape(lay.group, slots_all, 2 * chunk)
    held = lay.spread(pieces)
    units_moved = lax.ppermute(units_own, "expert", partner)
    units_held = jnp.where(my_flag, units_moved, units_own)
    units_held = lay.gathered(units_held)
    grads = weight_grads(held, units_held, chunk, units)
    return (layer_out, input_grad, gate_grad, grads[0][None], grads[1][None], grads[2][None])


def solution(mesh):
    placed = (
        P(("expert", "dp"), "tensor"),
        P(("expert", "dp"), None),
        P(("expert", "dp"), None),
        P(("expert", "dp"), "tensor"),
        P(),
        P(),
        P("expert", "dp", "tensor"),
        P("expert", "dp", "tensor"),
        P("expert", "dp", "tensor"),
    )


    return jax.shard_map(
        on_device,
        mesh=mesh,
        in_specs=placed,
        out_specs=(
            P(("expert", "dp"), "tensor"),
            P(("expert", "dp"), "tensor"),
            P(("expert", "dp"), None),
            P("expert", "dp", "tensor"),
            P("expert", "dp", "tensor"),
            P("expert", "dp", "tensor"),
        ),
        check_vma=False,
    )
```

```python
import jax
import jax.numpy as jnp
from jax import lax
from jax.experimental import pallas as pl
from jax.experimental.pallas import tpu as pltpu
from jax.sharding import PartitionSpec as P

CAP = 9
MAIN = 8
BF = jnp.bfloat16
F32 = jnp.float32
LANES = 128

contract = (((0,), (0,)), ((), ()))
inner = (((1,), (1,)), ((), ()))


def dot(a, b, dims):
    return lax.dot_general(a, b, dims, preferred_element_type=F32)


def pick(stack, index, count):
    return stack[0] if count == 1 else lax.dynamic_index_in_dim(stack, index, 0, keepdims=False)


class Layout:
    def __init__(self):
        self.n_d = lax.axis_size("dp")
        self.n_t = lax.axis_size("tensor")
        self.group = self.n_d // self.n_t
        self.d = lax.axis_index("dp")
        self.t = lax.axis_index("tensor")
        self.order = (self.d % self.group) * self.n_t + self.t

    def pairs(self, step):
        route = []
        for d in range(self.n_d):
            for t in range(self.n_t):
                half = d // self.group
                data = ((d % self.group) * self.n_t + t + step) % self.n_d
                route.append((data * self.n_t + half, d * self.n_t + t))
        return route

    def canonical(self, blocks):
        if self.group == 1:
            return blocks
        whole = jnp.stack(blocks)
        whole = jnp.take(whole, (jnp.arange(self.n_d) - self.order) % self.n_d, axis=0)
        return [whole[i] for i in range(self.n_d)]

    def spread(self, rows):
        blocks = []
        for step in range(self.n_d):
            target = (self.d - step) % self.n_d
            chunk = pick(rows, target // self.n_t, self.group)
            blocks.append(lax.ppermute(chunk, ("dp", "tensor"), self.pairs(step)))
        return self.canonical(blocks)

    def flipped(self, values):
        got = []
        for step in range(1, self.n_t):
            route = [(i, (i + step) % self.n_t) for i in range(self.n_t)]
            got.append(lax.ppermute(values[step - 1], "tensor", route))
        return got

    def others(self, value):
        got = []
        for step in range(1, self.n_d):
            route = [(i, (i + step) % self.n_d) for i in range(self.n_d)]
            got.append(lax.ppermute(value, "dp", route))
        return got

    def gathered(self, value):
        if self.n_d == 2 and self.group == 1:
            other = lax.ppermute(value, "dp", [(0, 1), (1, 0)])
            first = self.d == self.order
            return jnp.concatenate([jnp.where(first, value, other), jnp.where(first, other, value)])
        return lax.all_gather(value, "dp", axis=0, tiled=True)


def fold_width(cols):
    return -(-cols // (MAIN * LANES)) * LANES


def folded_shape(experts, cols):
    return shape((experts * MAIN, cols + fold_width(cols)), BF)


def fold(main, last, out):
    rows, cols = main.shape
    width = fold_width(cols)
    out[:, :cols] = main.astype(BF)
    row = lax.broadcasted_iota(jnp.int32, (rows, last.shape[0]), 0)
    col = lax.broadcasted_iota(jnp.int32, (rows, last.shape[0]), 1)
    repeat = jnp.where(row // MAIN == col, 1.0, 0.0).astype(BF)
    wide = jnp.dot(repeat, last.astype(BF), preferred_element_type=F32)
    place = lax.broadcasted_iota(jnp.int32, (rows, width), 0) % MAIN
    value = jnp.zeros((rows, width), F32)
    for q in range(cols // width):
        value = jnp.where(place == q, wide[:, q * width : (q + 1) * width], value)
    out[:, cols:] = value.astype(BF)


def unfold(tail, cols):
    rows, width = tail.shape
    experts = rows // MAIN
    row = lax.broadcasted_iota(jnp.int32, (experts, rows), 0)
    col = lax.broadcasted_iota(jnp.int32, (experts, rows), 1)
    pieces = []
    for q in range(cols // width):
        take = jnp.where(col == row * MAIN + q, 1.0, 0.0).astype(BF)
        pieces.append(jnp.dot(take, tail, preferred_element_type=F32))
    return jnp.concatenate(pieces, axis=1)


def exchanged(rows):
    return lax.all_to_all(rows, "expert", split_axis=0, concat_axis=0, tiled=True)


def call(kernel, outs, args, room, smem=0, far=0, scratch=(), flops=0):
    moved = sum(a.size * a.dtype.itemsize for a in args) + sum(
        o.size * o.dtype.itemsize for o in outs
    )
    return pl.pallas_call(
        kernel,
        out_shape=outs,
        in_specs=[pl.BlockSpec(memory_space=pltpu.SMEM)] * smem
        + [pl.BlockSpec(memory_space=pl.ANY)] * far
        + [pl.BlockSpec(memory_space=pltpu.VMEM)] * (len(args) - smem - far),
        out_specs=[pl.BlockSpec(memory_space=pltpu.VMEM)] * len(outs),
        scratch_shapes=scratch,
        compiler_params=pltpu.CompilerParams(vmem_limit_bytes=room),
        cost_estimate=pl.CostEstimate(flops=flops, bytes_accessed=moved, transcendentals=0),
    )(*args)


def room_for(*arrays):
    return (6 << 20) + 3 * sum(a.size * a.dtype.itemsize for a in arrays) // 2


def shape(dims, dtype):
    return jax.ShapeDtypeStruct(dims, dtype)


def wanted_column(placement, slots):
    row = lax.broadcasted_iota(jnp.int32, (slots, 1), 0)
    experts = slots // CAP
    main = row < experts * MAIN
    position = jnp.where(main, row // MAIN, row - experts * MAIN)
    wanted = jnp.zeros((slots, 1), jnp.int32)
    for e in range(experts):
        wanted = jnp.where(position == e, placement[e], wanted)
    return wanted, jnp.where(main, row % MAIN, MAIN)


def fetch(pairs, sems):
    copies = [pltpu.make_async_copy(x, y, sems.at[i]) for i, (x, y) in enumerate(pairs)]
    for copy in copies:
        copy.start()
    return copies


def head_kernel(*refs):
    given, (rows, select, weighted, other_side), kept = refs[:5], refs[5:9], refs[9:14]
    copies = fetch(zip(given, kept), refs[14])
    placement, routes, gates, tokens, cot = kept
    for copy in copies[:3]:
        copy.wait()
    slots, tok_count = select.shape
    top_count = routes.shape[0]
    wanted, slot = wanted_column(placement, slots)
    hit = jnp.zeros((slots, tok_count), F32)
    weight = jnp.zeros((slots, tok_count), F32)
    for k in range(top_count):
        match = routes[k : k + 1, :] == wanted
        hit = jnp.where(match, 1.0, hit)
        weight = jnp.where(match, gates[k : k + 1, :].astype(F32), weight)
    row_id = lax.broadcasted_iota(jnp.int32, (tok_count, tok_count), 0)
    col_id = lax.broadcasted_iota(jnp.int32, (tok_count, tok_count), 1)
    before = jnp.where(row_id < col_id, 1.0, 0.0).astype(BF)
    earlier = jnp.dot(hit.astype(BF), before, preferred_element_type=F32)
    live = (hit > 0.0) & (earlier == slot.astype(F32))
    chosen = jnp.where(live, 1.0, 0.0).astype(BF)
    scaled = jnp.where(live, weight, 0.0).astype(BF)
    select[...] = chosen
    weighted[...] = scaled
    copies[3].wait()
    x = jnp.dot(chosen, tokens[...], preferred_element_type=F32)
    copies[4].wait()
    d = jnp.dot(scaled, cot[...], preferred_element_type=F32)
    both = jnp.concatenate([x, d], axis=1)
    main = rows.shape[0]
    fold(both[:main], both[main:], rows)
    other_side[...] = rows[half_rows(rows, other=True)]


def half_rows(rows, other):
    count = rows.shape[0] // 2
    side = lax.axis_index("expert") // (lax.axis_size("expert") // 2)
    return pl.ds(pl.multiple_of((1 - side if other else side) * count, count), count)


def split_kernel(rows, x, d, my_side):
    main, half = rows.shape[0], x.shape[1]
    my_side[...] = rows[half_rows(rows, other=False)]
    last = unfold(rows[:, 2 * half :], 2 * half).astype(BF)
    for side, out in ((0, x), (1, d)):
        out[:main] = rows[:, side * half : (side + 1) * half]
        out[main:] = last[:, side * half : (side + 1) * half]


def held_kernel(flag, moved, near, own, out, both):
    main, cols = own.shape[0], out.shape[1]
    half = main // 2
    me = lax.axis_index("expert")
    mine = flag[me] != 1
    side = me // (lax.axis_size("expert") // 2)

    @pl.when(mine)
    def _():
        both[...] = own[...]

    @pl.when(jnp.logical_not(mine))
    def _():
        both[pl.ds(pl.multiple_of(side * half, half), half)] = near[...]
        both[pl.ds(pl.multiple_of((1 - side) * half, half), half)] = moved[...]

    out[:main] = both[:, :cols]
    out[main:] = unfold(both[:, cols:], cols).astype(BF)


class Rows:
    def __init__(self, n_d, n_t, own, others, kept):
        self.n_d, self.n_t, self.kept = n_d, n_t, kept
        self.group = n_d // n_t
        self.d, self.t = lax.axis_index("dp"), lax.axis_index("tensor")
        self.half = kept.shape[2]
        self.chunk = self.half // self.group
        kept[self.t] = own
        for s in range(1, n_t):
            kept[lax.rem(self.t - s + n_t, n_t)] = others[s - 1][...]

    def place(self, s):
        where = lax.rem(self.d - s + self.n_d, self.n_d)
        if self.group == 1:
            return where, slice(None)
        col = pl.multiple_of(lax.rem(where, self.group) * self.chunk, LANES)
        return where // self.group, pl.ds(col, self.chunk)

    def times(self, weight):
        value = None
        for s in range(self.n_d):
            side, cols = self.place(s)
            part = jnp.dot(self.kept[side, :, cols], weight(s), preferred_element_type=F32)
            value = part if value is None else value + part
        return value

    def store(self, s, term, results):
        side, cols = self.place(s)
        step = lax.rem(side - self.t + self.n_t, self.n_t)
        for k in range(self.n_t):

            @pl.when(step == k)
            def _():
                results[k][:, cols] = term.astype(BF)


class Weights:
    def __init__(self, n_d, shards, room, sems, order):
        self.n_d, self.room, self.waited = n_d, room, set()
        keys = [(which, s) for which in order for s in range(n_d)]
        pairs = [(shards[which * n_d + s], room.at[which, s]) for which, s in keys]
        self.copies = dict(zip(keys, fetch(pairs, sems)))

    def of(self, which):
        def shard(s):
            if (which, s) not in self.waited:
                self.copies[which, s].wait()
                self.waited.add((which, s))
            return self.room[which, s]

        return shard


def forward_kernel(n_d, n_t, *refs):
    shards, own, others = refs[: 3 * n_d], refs[3 * n_d], refs[3 * n_d + 1 : 3 * n_d + n_t]
    refs = refs[3 * n_d + n_t :]
    (gate_out, up_out, hidden_out), terms, (kept, room, sems) = refs[:3], refs[3:-3], refs[-3:]
    weights = Weights(n_d, shards, room, sems, (0, 1, 2))
    rows = Rows(n_d, n_t, own[...], others, kept)
    gate, up = rows.times(weights.of(0)), rows.times(weights.of(1))
    hidden = (gate * jax.nn.sigmoid(gate) * up).astype(BF)
    gate_out[...], up_out[...], hidden_out[...] = gate, up, hidden
    down = weights.of(2)
    for s in range(n_d):
        rows.store(s, dot(hidden, down(s), inner), terms)


def backward_kernel(n_d, n_t, *refs):
    shards, own, others = refs[: 3 * n_d], refs[3 * n_d], refs[3 * n_d + 1 : 3 * n_d + n_t]
    refs = refs[3 * n_d + n_t :]
    (gate_in, up_in, hidden_in, units_out), terms = refs[:4], refs[4:-3]
    kept, room, sems = refs[-3:]
    weights = Weights(n_d, shards, room, sems, (2, 0, 1))
    rows = Rows(n_d, n_t, own[...], others, kept)
    d_hidden = rows.times(weights.of(2))
    gate, up = gate_in[...], up_in[...]
    sig = jax.nn.sigmoid(gate)
    d_gate = (d_hidden * up * sig * (1.0 + gate * (1.0 - sig))).astype(BF)
    d_up = (d_hidden * gate * sig).astype(BF)
    units = gate.shape[1]
    units_out[:, :units] = d_gate
    units_out[:, units : 2 * units] = d_up
    units_out[:, 2 * units :] = hidden_in[...]
    by_gate = [dot(d_gate, weights.of(0)(s), inner) for s in range(n_d)]
    for s in range(n_d):
        rows.store(s, by_gate[s] + dot(d_up, weights.of(1)(s), inner), terms)


def home_kernel(*refs):
    home = refs[-1]
    count = (len(refs) - 1) // 2
    sides = []
    for side in range(2):
        value = None
        for ref in refs[side * count : (side + 1) * count]:
            part = ref[...].astype(F32)
            value = part if value is None else value + part
        sides.append(value)
    both = jnp.concatenate(sides, axis=1)
    main = home.shape[0]
    fold(both[:main], both[main:], home)


def gate_kernel(placement, routes, select, cot, back, gate_part):
    slots = select.shape[0]
    half = cot.shape[1]
    wanted, _ = wanted_column(placement, slots)
    last = unfold(back[:, 2 * half :], 2 * half)[:, :half].astype(BF)
    scores = jnp.concatenate([dot(back[:, :half], cot[...], inner), dot(last, cot[...], inner)])
    scores = jnp.where(select[...].astype(F32) > 0.0, scores, 0.0)
    for k in range(routes.shape[0]):
        match = routes[k : k + 1, :] == wanted
        gate_part[k : k + 1, :] = jnp.sum(
            jnp.where(match, scores, 0.0), axis=0, keepdims=True
        )


def combine_kernel(select, weighted, back, layer_out, input_grad):
    main, half = back.shape[0], layer_out.shape[1]
    last = unfold(back[:, 2 * half :], 2 * half).astype(BF)
    for side, weight, out in ((0, weighted, layer_out), (1, select, input_grad)):
        cols = slice(side * half, (side + 1) * half)
        value = dot(weight[:main], back[:, cols], contract)
        out[...] = (value + dot(weight[main:], last[:, cols], contract)).astype(BF)


def grads_kernel(count, *refs):
    held, kept_units, (g_gate, g_up, g_down) = refs[: 2 * count], refs[2 * count], refs[-3:]
    units = g_gate.shape[1]

    def joined(blocks):
        return jnp.concatenate([x[...].astype(F32) for x in blocks]).astype(BF)

    both = dot(joined(held[:count]), kept_units[:, : 2 * units], contract).astype(BF)
    g_gate[...] = both[:, :units]
    g_up[...] = both[:, units:]
    g_down[...] = dot(joined(held[count:]), kept_units[:, 2 * units :], contract).astype(BF)


def weight_grads(held, units_held, chunk, units):
    count, rows = len(held), held[0].shape[0]
    block = next(b for b in (896, 512, 256, LANES) if chunk % b == 0)
    steps = chunk // block
    out = shape((chunk, units), BF)
    spec = pl.BlockSpec((block, units), lambda i: (i, 0))
    x_spec = pl.BlockSpec((rows, block), lambda i: (0, i))
    d_spec = pl.BlockSpec((rows, block), lambda i: (0, i + steps))
    return pl.pallas_call(
        lambda *refs: grads_kernel(count, *refs),
        grid=(steps,),
        out_shape=[out] * 3,
        in_specs=[x_spec] * count
        + [d_spec] * count
        + [pl.BlockSpec((count * rows, 3 * units), lambda i: (0, 0))],
        out_specs=[spec] * 3,
        compiler_params=pltpu.CompilerParams(
            vmem_limit_bytes=(12 << 20) + 6 * count * rows * 2 * (3 * units + 2 * block)
        ),
        cost_estimate=pl.CostEstimate(
            flops=6 * count * rows * chunk * units,
            bytes_accessed=6 * chunk * units,
            transcendentals=0,
        ),
        name="weight_grads",
    )(*held, *held, units_held)


def on_device(tokens, routes, gates, cotangent, placement, swap_flag, w_gate, w_up, w_down):
    experts = lax.axis_size("expert")
    myself = lax.axis_index("expert")
    lay = Layout()
    places = jnp.arange(experts, dtype=jnp.int32)
    my_flag = jnp.sum(jnp.where(places == myself, swap_flag, 0)) == 1
    wg, wu, wd = w_gate[0], w_up[0], w_down[0]
    chunk, units = wg.shape
    tok_count, top_count = routes.shape
    slots_all = experts * CAP
    half_width = tokens.shape[1]
    routes_t, gates_t = routes.T, gates.T

    folded = folded_shape(experts, 2 * half_width)
    outs = [
        folded,
        shape((slots_all, tok_count), BF),
        shape((slots_all, tok_count), BF),
        shape((folded.shape[0] // 2, folded.shape[1]), BF),
    ]
    given = (placement, routes_t, gates_t, tokens, cotangent)
    outgoing, select, weighted, other_side = call(
        head_kernel,
        outs,
        given,
        None,
        far=len(given),
        scratch=[
            pltpu.SMEM(placement.shape, jnp.int32),
            *(pltpu.VMEM(x.shape, x.dtype) for x in given[1:]),
            pltpu.SemaphoreType.DMA((len(given),)),
        ],
    )
    arrived = exchanged(outgoing)
    half_axis = experts // 2
    near = lax.all_to_all(
        other_side,
        "expert",
        split_axis=0,
        concat_axis=0,
        axis_index_groups=[list(range(half_axis)), list(range(half_axis, experts))],
        tiled=True,
    )
    sides = [shape((slots_all, half_width), BF)] * 2 + [shape(other_side.shape, BF)]
    x_own, d_own, my_side = call(split_kernel, sides, (arrived,), room_for(*sides, *sides))
    own_weights = (wg, wu, wd)
    shards = []
    for own in own_weights:
        shards += [own, *lay.others(own)]
    x_other = lay.flipped([x_own] * (lay.n_t - 1))
    d_other = lay.flipped([d_own] * (lay.n_t - 1))
    term = shape((slots_all, half_width), BF)
    kept = [
        pltpu.VMEM((lay.n_t, slots_all, half_width), BF),
        pltpu.VMEM((3, lay.n_d, chunk, units), BF),
        pltpu.SemaphoreType.DMA((3 * lay.n_d,)),
    ]
    outs = [shape((slots_all, units), F32)] * 2 + [shape((slots_all, units), BF)]
    room = 52 << 20
    work = 6 * slots_all * lay.n_d * chunk * units
    gate, up, hidden, *out_terms = call(
        lambda *refs: forward_kernel(lay.n_d, lay.n_t, *refs),
        outs + [term] * lay.n_t,
        (*shards, x_own, *x_other),
        room,
        scratch=kept,
        far=len(shards),
        flops=work,
    )
    units_own, *in_terms = call(
        lambda *refs: backward_kernel(lay.n_d, lay.n_t, *refs),
        [shape((slots_all, 3 * units), BF)] + [term] * lay.n_t,
        (*shards, d_own, *d_other, gate, up, hidden),
        room,
        scratch=kept,
        far=len(shards),
        flops=work,
    )
    out_got = [out_terms[0], *lay.flipped(out_terms[1:])]
    in_got = [in_terms[0], *lay.flipped(in_terms[1:])]
    (home,) = call(
        home_kernel,
        [folded_shape(experts, 2 * half_width)],
        (*out_got, *in_got),
        room_for(*out_got, *in_got, *out_got, *in_got),
    )
    back = exchanged(home)

    gate_shape = shape((top_count, tok_count), F32)
    (gate_part,) = call(
        gate_kernel,
        [gate_shape],
        (placement, routes_t, select, cotangent, back),
        room_for(cotangent, back),
        smem=1,
    )
    gate_grad = gate_part
    for step in range(1, lay.n_t):
        other = lax.ppermute(
            gate_part, "tensor", [(i, (i + step) % lay.n_t) for i in range(lay.n_t)]
        )
        gate_grad = gate_grad + other
    gate_grad = gate_grad.T
    outs = [shape(tokens.shape, BF)] * 2
    layer_out, input_grad = call(
        combine_kernel, outs, (select, weighted, back), room_for(back, *outs)
    )

    partner = [(i, (i + experts // 2) % experts) for i in range(experts)]
    moved = lax.ppermute(my_side, "expert", partner)
    both = shape((slots_all, 2 * half_width), BF)
    (held,) = call(
        held_kernel,
        [both],
        (swap_flag, moved, near, arrived),
        room_for(both, both, both, both),
        smem=1,
        scratch=[pltpu.VMEM(arrived.shape, BF)],
    )
    if lay.group == 1:
        pieces = held[None]
    else:
        pieces = jnp.moveaxis(held.reshape(slots_all, 2, lay.group, chunk), 2, 0)
        pieces = pieces.reshape(lay.group, slots_all, 2 * chunk)
    held = lay.spread(pieces)
    units_moved = lax.ppermute(units_own, "expert", partner)
    units_held = jnp.where(my_flag, units_moved, units_own)
    units_held = lay.gathered(units_held)
    grads = weight_grads(held, units_held, chunk, units)
    return (layer_out, input_grad, gate_grad, grads[0][None], grads[1][None], grads[2][None])


def solution(mesh):
    placed = (
        P(("expert", "dp"), "tensor"),
        P(("expert", "dp"), None),
        P(("expert", "dp"), None),
        P(("expert", "dp"), "tensor"),
        P(),
        P(),
        P("expert", "dp", "tensor"),
        P("expert", "dp", "tensor"),
        P("expert", "dp", "tensor"),
    )


    return jax.shard_map(
        on_device,
        mesh=mesh,
        in_specs=placed,
        out_specs=(
            P(("expert", "dp"), "tensor"),
            P(("expert", "dp"), "tensor"),
            P(("expert", "dp"), None),
            P("expert", "dp", "tensor"),
            P("expert", "dp", "tensor"),
            P("expert", "dp", "tensor"),
        ),
        check_vma=False,
    )
```
